32 devices in a mesh: wide: 16 (over z, x, core), seq: 2 (over y).
Axes of the slice: x: 2, y: 2, z: 4, core: 2. Of those that a mesh axis runs over, the one named last changes fastest.
Arguments:
- latents: bfloat16 [208, 128, 1152], P('wide', 'seq'), may hold values from -6 to 6
- skip_store: bfloat16 [208, 128, 1152], P('wide', None, 'seq'), may hold values from -6 to 6
- lengths: int32 [208], P('wide'), may hold values from 80 to 128, as said below
- cotangent: bfloat16 [208, 128, 1152], P('wide', 'seq'), may hold values from -6 to 6
- skip_weight: bfloat16 [2304, 1152], P('seq'), may hold values from -0.125 to 0.125
- skip_bias: bfloat16 [1152], P('seq'), may hold values from -1.75 to 1.75
- first_gain: bfloat16 [1152], P('seq'), may hold values from 0.099609375 to 1.8984375
- first_shift: bfloat16 [1152], P('seq'), may hold values from -1.75 to 1.75
- inward_weight: bfloat16 [1152, 3456], P('seq'), may hold values from -0.1875 to 0.1875
- outward_weight: bfloat16 [1152, 1152], P('seq'), may hold values from -0.5 to 0.5
- outward_bias: bfloat16 [1152], P('seq'), may hold values from -1.75 to 1.75
- second_gain: bfloat16 [1152], P('seq'), may hold values from 0.099609375 to 1.8984375
- second_shift: bfloat16 [1152], P('seq'), may hold values from -1.75 to 1.75
- expand_weight: bfloat16 [1152, 4608], P('seq'), may hold values from -0.1875 to 0.1875
- expand_bias: bfloat16 [4608], P('seq'), may hold values from -1.75 to 1.75
- contract_weight: bfloat16 [4608, 1152], P('seq'), may hold values from -0.09375 to 0.09375
- contract_bias: bfloat16 [1152], P('seq'), may hold values from -1.75 to 1.75
Outputs:
- output: bfloat16 [208, 128, 1152], P('wide', 'seq')
- latents_grad: float32 [208, 128, 1152], P('wide', 'seq')
- skip_grad: bfloat16 [208, 128, 1152], P('wide', None, 'seq')
- skip_weight_grad: float32 [2304, 1152], P('seq')
- skip_bias_grad: float32 [1152], P('seq')
- first_gain_grad: float32 [1152], P('seq')
- first_shift_grad: float32 [1152], P('seq')
- inward_weight_grad: float32 [1152, 3456], P('seq')
- outward_weight_grad: float32 [1152, 1152], P('seq')
- outward_bias_grad: float32 [1152], P('seq')
- second_gain_grad: float32 [1152], P('seq')
- second_shift_grad: float32 [1152], P('seq')
- expand_weight_grad: float32 [1152, 4608], P('seq')
- expand_bias_grad: float32 [4608], P('seq')
- contract_weight_grad: float32 [4608, 1152], P('seq')
- contract_bias_grad: float32 [1152], P('seq')
The draws below stay inside these ranges and needn't reach their ends.
Inputs may be any that keep to these rules, and one draw needn't show every extreme that they name: `lengths`: among the 13 items of each index of wide, at least one has all 128 slots live.
All inputs are finite; a program needn't handle non-finite values.
Results may differ from the reference program's by a relative error of at most 0.02.
Values may be sent and summed in bfloat16 or wider, within the bound.
No kernel may reach another device: no remote copies, remote signals or barrier semaphores. Data moves between devices by JAX's collectives and lax.ppermute only.
A program may use at most 512 MiB of HBM per device.

```python
import jax
import jax.numpy as jnp
from jax import lax

D = 1152
HEADS = 16
HEAD_DIM = 72
FF = 4608
ITEMS = 13
SLOT = 128
ITEMS_ALL = 208


def draw_lengths(key, part):
    least_len = SLOT * 5 // 8
    drawn_len = jax.random.randint(jax.random.fold_in(key, 11), (ITEMS_ALL,), least_len, SLOT + 1)
    chosen = jax.random.randint(jax.random.fold_in(key, 12), (ITEMS_ALL // ITEMS,), 0, ITEMS)
    filled = jnp.arange(ITEMS_ALL) % ITEMS == jnp.repeat(chosen, ITEMS)
    return jnp.where(filled, SLOT, drawn_len).astype(jnp.int32)


def levels(own_key, extent, split, smallest, high):
    def one(position, shards_of):
        steps = jax.random.uniform(jax.random.fold_in(jax.random.fold_in(own_key, 6), position), (shards_of,), jnp.float32, smallest / len(split), high / len(split))
        return jnp.repeat(jnp.exp(steps), extent[position] // shards_of).reshape((-1,) + (1,) * (len(extent) - position - 1))

    level = one(*split[0])
    for cut in split[1:]:
        level = level * one(*cut)
    return level


def bell_draw(rng, extent, width, bound, cuts=(), kind=jnp.bfloat16):
    entries = width * jax.random.normal(rng, extent, jnp.float32)
    if cuts:
        entries = entries * levels(rng, extent, cuts, -0.22, 0.18)
    return jnp.clip(entries, -bound, bound).astype(kind)


def setup_inputs(seed: int = 0) -> dict:
    seeds = jax.random.split(jax.random.key(seed), 18)
    latents = bell_draw(seeds[0], (ITEMS_ALL, SLOT, D), 1.0, 6.0, ((0, 16), (1, 2)))
    skip_store = bell_draw(seeds[1], (ITEMS_ALL, SLOT, D), 1.0, 6.0, ((0, 16), (2, 2)))
    lengths = draw_lengths(jax.random.fold_in(seeds[17], 71), 0)
    cotangent = bell_draw(seeds[3], (ITEMS_ALL, SLOT, D), 1.0, 6.0, ((0, 16), (1, 2)))
    skip_weight = bell_draw(seeds[4], (2 * D, D), (2 * D) ** -0.5, 0.125, ((0, 2),))
    skip_bias = bell_draw(seeds[5], (D,), 0.3, 1.75, ((0, 2),))
    first_gain = jnp.clip(1.0 + 0.18 * jax.random.normal(seeds[6], (D,), jnp.float32), 0.099609375, 1.8984375).astype(jnp.bfloat16)
    first_shift = bell_draw(seeds[7], (D,), 0.3, 1.75, ((0, 2),))
    inward_weight = bell_draw(seeds[8], (D, 3 * D), D ** -0.5, 0.1875, ((0, 2),))
    outward_weight = bell_draw(seeds[9], (D, D), (D // 8) ** -0.5, 0.5, ((0, 2),))
    outward_bias = bell_draw(seeds[10], (D,), 0.3, 1.75, ((0, 2),))
    second_gain = jnp.clip(1.0 + 0.18 * jax.random.normal(seeds[11], (D,), jnp.float32), 0.099609375, 1.8984375).astype(jnp.bfloat16)
    second_shift = bell_draw(seeds[12], (D,), 0.3, 1.75, ((0, 2),))
    expand_weight = bell_draw(seeds[13], (D, FF), D ** -0.5, 0.1875, ((0, 2),))
    expand_bias = bell_draw(seeds[14], (FF,), 0.3, 1.75, ((0, 2),))
    contract_weight = bell_draw(seeds[15], (FF, D), FF ** -0.5, 0.09375, ((0, 2),))
    contract_bias = bell_draw(seeds[16], (D,), 0.3, 1.75, ((0, 2),))
    return dict(latents=latents, skip_store=skip_store, lengths=lengths, cotangent=cotangent, skip_weight=skip_weight, skip_bias=skip_bias, first_gain=first_gain, first_shift=first_shift, inward_weight=inward_weight, outward_weight=outward_weight, outward_bias=outward_bias, second_gain=second_gain, second_shift=second_shift, expand_weight=expand_weight, expand_bias=expand_bias, contract_weight=contract_weight, contract_bias=contract_bias)


EPS = 1e-05
NEG = -1e+30

@jax.custom_vjp
def low(v):
    return lax.optimization_barrier(v.astype(jnp.bfloat16)).astype(jnp.float32)

@jax.custom_vjp
def low_back(v):
    return v

def low_keep(v):
    return (low(v), None)

def low_pass(kept, grad):
    return (grad,)

def back_keep(v):
    return (v, None)

def back_low(kept, grad):
    return (low(grad),)
low.defvjp(low_keep, low_pass)
low_back.defvjp(back_keep, back_low)

def product(left_side, right_side):
    return jnp.dot(left_side, right_side, precision=lax.Precision.HIGHEST)

def layer_norm(hidden, gain, shift):
    mean_val = lax.optimization_barrier(jnp.mean(hidden, -1, keepdims=True))
    centred = hidden - mean_val
    var_val = lax.optimization_barrier(jnp.mean(centred * centred, -1, keepdims=True))
    return centred * lax.rsqrt(var_val + EPS) * gain + shift

def group_forward(params, latent_in, skip_in, key_valid):
    skip_weight, skip_bias, first_gain, first_shift, inward_weight, outward_weight, outward_bias, second_gain, second_shift, expand_weight, expand_bias, contract_weight, contract_bias = params
    item_count, slot_count, model_width = latent_in.shape
    row_count = item_count * slot_count
    skip_in = low_back(skip_in)
    joined = jnp.concatenate([latent_in, skip_in], -1).reshape(row_count, 2 * model_width)
    base = low_back(product(joined, skip_weight) + skip_bias)
    first_normed = low(layer_norm(base, first_gain, first_shift))
    qkv_vals = low_back(low(product(first_normed, inward_weight)))
    qkv_vals = qkv_vals.reshape(item_count, slot_count, 3, HEADS, HEAD_DIM)
    queries = qkv_vals[:, :, 0]
    keys_all = qkv_vals[:, :, 1]
    values_all = qkv_vals[:, :, 2]
    scores = jnp.einsum('iqhd,ikhd->ihqk', queries, keys_all, precision=lax.Precision.HIGHEST)
    scores = low_back(scores * HEAD_DIM ** (-0.5))
    scores = jnp.where(key_valid[:, None, None, :], scores, NEG)
    probs = low(jax.nn.softmax(scores, -1))
    mixed = jnp.einsum('ihqk,ikhd->iqhd', probs, values_all, precision=lax.Precision.HIGHEST)
    mixed = low_back(low(mixed.reshape(row_count, model_width)))
    middle = base + low_back(product(mixed, outward_weight) + outward_bias)
    second_normed = low(layer_norm(middle, second_gain, second_shift))
    upper = low_back(product(second_normed, expand_weight) + expand_bias)
    activated = low(jax.nn.gelu(upper, approximate=False))
    result = middle + low_back(product(activated, contract_weight) + contract_bias)
    return result.reshape(item_count, slot_count, model_width)

def to_float(tensor):
    return tensor.astype(jnp.float32)

def reference(latents, skip_store, lengths, cotangent, skip_weight, skip_bias, first_gain, first_shift, inward_weight, outward_weight, outward_bias, second_gain, second_shift, expand_weight, expand_bias, contract_weight, contract_bias):
    params = tuple((to_float(tensor) for tensor in (skip_weight, skip_bias, first_gain, first_shift, inward_weight, outward_weight, outward_bias, second_gain, second_shift, expand_weight, expand_bias, contract_weight, contract_bias)))
    group_count = ITEMS_ALL // ITEMS

    def grouped(tensor):
        return tensor.reshape((group_count, ITEMS) + tensor.shape[1:])
    key_valid = jnp.arange(SLOT, dtype=jnp.int32)[None, :] < lengths.astype(jnp.int32)[:, None]

    def forward(weights, latent_in, skip_in):

        def advance(running, member):
            return (running, jax.checkpoint(group_forward)(weights, member[0], member[1], member[2]))
        running, stacked = lax.scan(advance, jnp.zeros((), jnp.float32), (latent_in, skip_in, grouped(key_valid)))
        return stacked
    stacked, pullback = jax.vjp(forward, params, grouped(to_float(latents)), grouped(to_float(skip_store)))
    grad_params, grad_latent, grad_skipped = pullback(grouped(to_float(cotangent)))
    output = stacked.reshape(ITEMS_ALL, SLOT, D).astype(jnp.bfloat16)
    grad_latent = grad_latent.reshape(ITEMS_ALL, SLOT, D)
    grad_skipped = grad_skipped.reshape(ITEMS_ALL, SLOT, D).astype(jnp.bfloat16)
    g_skipw, g_skipb, g_gain1, g_shift1, g_inward, g_outward, g_outb, g_gain2, g_shift2, g_expand, g_expandb, g_contract, g_contractb = grad_params
    return (output, grad_latent, grad_skipped, g_skipw, g_skipb, g_gain1, g_shift1, g_inward, g_outward, g_outb, g_gain2, g_shift2, g_expand, g_expandb, g_contract, g_contractb)
```

```python
import jax
import jax.numpy as jnp
from jax import lax
from jax.sharding import Mesh
from jax.sharding import PartitionSpec as P

HEAD_DIM = 72

EPS = 1e-05
NEG = -1e30
WIDE = ("z", "x", "c")
BF16 = jnp.bfloat16
F32 = jnp.float32


def across(left_side, right_side):
    return lax.dot_general(
        left_side, right_side, (((0,), (0,)), ((), ())), preferred_element_type=F32
    )


def against(left_side, right_side):
    return lax.dot_general(
        left_side, right_side, (((1,), (1,)), ((), ())), preferred_element_type=F32
    )


def simple(left_side, right_side):
    return jnp.dot(left_side, right_side, preferred_element_type=F32)


def pick(array, index, size, axis=0):
    return lax.dynamic_slice_in_dim(array, index * size, size, axis)


def flip(array, axis):
    return lax.ppermute(array, axis, [(0, 1), (1, 0)])


def ordered(mine, other, index, axis=0):
    return jnp.where(
        index == 0,
        jnp.concatenate([mine, other], axis),
        jnp.concatenate([other, mine], axis),
    )


def fast_mesh():
    return lax.axis_size("seq") == 2 and lax.axis_size("z") == 4


def gather_weight(shard):
    if not fast_mesh():
        return lax.all_gather(shard, "seq", axis=0, tiled=True)
    place = lax.axis_index("x") * 2 + lax.axis_index("c")
    quarter = pick(shard, place, shard.shape[0] // 4)
    other = lax.all_gather(flip(quarter, "seq"), ("x", "c"), axis=0, tiled=True)
    return ordered(shard, other, lax.axis_index("seq"))


def reduce_weight(grad, after=None):
    if not fast_mesh():
        part = lax.psum_scatter(
            grad.astype(BF16), "seq", scatter_dimension=0, tiled=True
        )
        return lax.psum(part, WIDE).astype(F32)
    rows, columns = grad.shape
    core, side = lax.axis_index("c"), lax.axis_index("seq")
    blocks = grad.astype(BF16).reshape(2, 2, rows // 4, columns)

    def block(array, index, axis):
        return lax.dynamic_index_in_dim(array, index, axis, keepdims=False)

    def add(left, right):
        return (left.astype(F32) + right.astype(F32)).astype(BF16)

    chip = add(block(blocks, core, 1), flip(block(blocks, 1 - core, 1), "c"))
    part = add(block(chip, side, 0), flip(block(chip, 1 - side, 0), "seq"))
    if after is not None:
        part, after = lax.optimization_barrier((part, after))
    part = lax.psum(part, ("z", "x"))
    return ordered(part, flip(part, "c"), core).astype(F32)


def gather_vectors(vectors):
    joined = jnp.concatenate(vectors)
    count = joined.shape[0]
    if fast_mesh():
        mine = joined.reshape(1, count)
        everything = ordered(mine, flip(mine, "seq"), lax.axis_index("seq"))
    else:
        everything = lax.all_gather(joined.reshape(1, count), "seq", axis=0, tiled=True)
    out, start = [], 0
    for vector in vectors:
        size = vector.shape[0]
        out.append(everything[:, start : start + size].reshape(-1).astype(F32))
        start += size
    return out


def reduce_vectors(vectors):
    ways = lax.axis_size("seq")
    side = lax.axis_index("seq")
    joined = jnp.concatenate(vectors)
    if fast_mesh():
        joined = jnp.concatenate([joined, jnp.zeros((-joined.shape[0]) % 16384, F32)])
        parts = lax.all_gather(joined.reshape(-1, 1024), WIDE + ("seq",), axis=0)
        total = jnp.sum(parts, 0).reshape(-1)
    else:
        total = lax.psum(joined, WIDE + ("seq",))
    out, start = [], 0
    for vector in vectors:
        size = vector.shape[0] // ways
        out.append(lax.dynamic_slice_in_dim(total, start + side * size, size, 0))
        start += vector.shape[0]
    return out


def share_items(array, per, axis):
    ways, side = lax.axis_size("seq"), lax.axis_index("seq")
    items, size = array.shape[0], array.shape[axis]
    array = jnp.pad(array, [(0, per * ways - items)] + [(0, 0)] * (array.ndim - 1))
    shape = list(array.shape)
    shape[0], shape[axis] = per, size * ways
    whole = jnp.zeros(shape, array.dtype)
    for hop in range(ways):
        piece = pick(array, (side + hop) % ways, per)
        if hop:
            piece = lax.ppermute(
                piece, "seq", [(i, (i + hop) % ways) for i in range(ways)]
            )
        source = (side - hop) % ways
        whole = lax.dynamic_update_slice_in_dim(whole, piece, source * size, axis)
    return whole


def return_items(whole, items, axis):
    ways, side = lax.axis_size("seq"), lax.axis_index("seq")
    per, size = whole.shape[0], whole.shape[axis] // ways
    shape = list(whole.shape)
    shape[0], shape[axis] = per * ways, size
    array = jnp.zeros(shape, whole.dtype)
    for hop in range(ways):
        piece = pick(whole, (side + hop) % ways, size, axis)
        if hop:
            piece = lax.ppermute(
                piece, "seq", [(i, (i + hop) % ways) for i in range(ways)]
            )
        source = (side - hop) % ways
        array = lax.dynamic_update_slice_in_dim(array, piece, source * per, 0)
    return array[:items]


def normalize(hidden):
    mean_val = jnp.mean(hidden, -1, keepdims=True)
    centred = hidden - mean_val
    scale = lax.rsqrt(jnp.mean(centred * centred, -1, keepdims=True) + EPS)
    return centred * scale, scale


def norm_back(grad, hidden, gain):
    xhat, scale = normalize(hidden)
    inner = grad * gain
    back = scale * (
        inner
        - jnp.mean(inner, -1, keepdims=True)
        - xhat * jnp.mean(inner * xhat, -1, keepdims=True)
    )
    return back, jnp.sum(grad * xhat, 0), jnp.sum(grad, 0)


def masked_scores(queries, keys_all, key_valid, score_scale):
    scores = (
        jnp.einsum("iqhd,ikhd->ihqk", queries, keys_all, preferred_element_type=F32)
        * score_scale
    )
    return jnp.where(key_valid[:, None, None, :], scores, NEG)


def attend(queries, keys_all, values_all, key_valid, score_scale):
    scores = masked_scores(queries, keys_all, key_valid, score_scale)
    peak = jnp.max(scores, -1, keepdims=True)
    raised = jnp.exp(scores - peak)
    total = jnp.sum(raised, -1, keepdims=True)
    probs = (raised / total).astype(BF16)
    mixed = jnp.einsum("ihqk,ikhd->iqhd", probs, values_all, preferred_element_type=F32)
    return (mixed.astype(BF16), peak + jnp.log(total))


def attend_back(queries, keys_all, values_all, key_valid, score_scale, log_total, grad_mixed):
    scores = masked_scores(queries, keys_all, key_valid, score_scale)
    probs = jnp.exp(scores - log_total)
    grad_probs = jnp.einsum(
        "iqhd,ikhd->ihqk", grad_mixed, values_all, preferred_element_type=F32
    )
    grad_scores = probs * (grad_probs - jnp.sum(grad_probs * probs, -1, keepdims=True))
    grad_scores = grad_scores.astype(BF16)
    grad_query = (
        jnp.einsum("ihqk,ikhd->iqhd", grad_scores, keys_all, preferred_element_type=F32)
        * score_scale
    )
    grad_key = (
        jnp.einsum("ihqk,iqhd->ikhd", grad_scores, queries, preferred_element_type=F32)
        * score_scale
    )
    grad_value = jnp.einsum(
        "ihqk,iqhd->ikhd", probs.astype(BF16), grad_mixed, preferred_element_type=F32
    )
    return (grad_query, grad_key, grad_value)


def gelu_pair(upper):
    below = 0.5 * (1.0 + lax.erf(upper * 0.7071067811865476))
    bell = jnp.exp(-0.5 * upper * upper) * 0.3989422804014327
    return (upper * below).astype(BF16), (below + upper * bell).astype(BF16)


def per_device(
    latents,
    skip_store,
    lengths,
    cotangent,
    skip_weight,
    skip_bias,
    first_gain,
    first_shift,
    inward_weight,
    outward_weight,
    outward_bias,
    second_gain,
    second_shift,
    expand_weight,
    expand_bias,
    contract_weight,
    contract_bias,
):
    items, slot_dev, width = latents.shape
    ways, side = lax.axis_size("seq"), lax.axis_index("seq")
    slots = slot_dev * ways
    per = -(-items // ways)
    rows = per * slots
    heads = width // HEAD_DIM
    score_scale = HEAD_DIM ** (-0.5)

    live = jnp.pad(lengths, (0, per * ways - items), constant_values=slots)
    live = pick(live, side, per)
    key_valid = jnp.arange(slots, dtype=jnp.int32)[None, :] < live[:, None]

    skip_rows = share_items(skip_store, per, 2)
    latent_rows = share_items(latents, per, 1)
    skip_matrix = gather_weight(skip_weight)
    (
        skip_offset,
        gain_first,
        shift_first,
        outward_offset,
        gain_second,
        shift_second,
        expand_offset,
        contract_offset,
    ) = gather_vectors(
        (
            skip_bias,
            first_gain,
            first_shift,
            outward_bias,
            second_gain,
            second_shift,
            expand_bias,
            contract_bias,
        )
    )
    inward_matrix = gather_weight(inward_weight)
    outward_matrix = gather_weight(outward_weight)
    expand_matrix = gather_weight(expand_weight)
    contract_matrix = gather_weight(contract_weight)
    grad_out = share_items(cotangent, per, 1).reshape(rows, width)

    joined = jnp.concatenate([latent_rows, skip_rows], -1).reshape(rows, 2 * width)
    base = simple(joined, skip_matrix) + skip_offset
    first_normed = (normalize(base)[0] * gain_first + shift_first).astype(BF16)
    qkv_vals = simple(first_normed, inward_matrix).astype(BF16)
    qkv_split = qkv_vals.reshape(per, slots, 3, heads, HEAD_DIM)
    queries, keys_all, values_all = (qkv_split[:, :, i] for i in range(3))
    mixed, log_total = attend(queries, keys_all, values_all, key_valid, score_scale)
    mixed_rows = mixed.reshape(rows, width)
    middle = base + simple(mixed_rows, outward_matrix) + outward_offset
    second_normed = (normalize(middle)[0] * gain_second + shift_second).astype(BF16)
    upper = simple(second_normed, expand_matrix) + expand_offset
    activated, slope = lax.optimization_barrier(gelu_pair(upper))
    result = middle + simple(activated, contract_matrix) + contract_offset
    output = return_items(result.astype(BF16).reshape(per, slots, width), items, 1)

    sum_contract = reduce_weight(across(activated, grad_out))
    grad_result = grad_out.astype(F32)
    grad_contract_off = jnp.sum(grad_result, 0)
    grad_act = against(grad_out, contract_matrix)
    grad_upper = (grad_act * slope.astype(F32)).astype(BF16)
    sum_expand = reduce_weight(across(second_normed, grad_upper), sum_contract)
    grad_expand_off = jnp.sum(grad_upper.astype(F32), 0)
    grad_second = against(grad_upper, expand_matrix)
    grad_mid_ln, grad_gain_two, grad_shift_two = norm_back(
        grad_second, middle, gain_second
    )
    grad_middle = grad_result + grad_mid_ln
    grad_branch = grad_middle.astype(BF16)
    sum_outward = reduce_weight(across(mixed_rows, grad_branch), sum_expand)
    grad_outward_off = jnp.sum(grad_branch.astype(F32), 0)
    grad_mixed = against(grad_branch, outward_matrix).astype(BF16)
    grad_heads = grad_mixed.reshape(per, slots, heads, HEAD_DIM)
    grad_qkv = jnp.stack(
        attend_back(
            queries, keys_all, values_all, key_valid, score_scale, log_total, grad_heads
        ),
        2,
    ).astype(BF16)
    grad_qkv = grad_qkv.reshape(rows, 3 * width)
    sum_inward = reduce_weight(across(first_normed, grad_qkv), sum_outward)
    grad_first = against(grad_qkv, inward_matrix)
    grad_base_ln, grad_gain_one, grad_shift_one = norm_back(
        grad_first, base, gain_first
    )
    grad_base = (grad_middle + grad_base_ln).astype(BF16)
    sum_skipw = reduce_weight(across(joined, grad_base), sum_inward)
    grad_skip_off = jnp.sum(grad_base.astype(F32), 0)
    grad_joined = against(grad_base, skip_matrix).astype(BF16)
    grad_joined = grad_joined.reshape(per, slots, 2 * width)
    grad_latents = return_items(grad_joined[:, :, :width], items, 1).astype(F32)
    grad_skip = return_items(grad_joined[:, :, width:], items, 2)
    (
        sum_skipb,
        sum_gain1,
        sum_shift1,
        sum_outb,
        sum_gain2,
        sum_shift2,
        sum_expandb,
        sum_contractb,
    ) = reduce_vectors(
        (
            grad_skip_off,
            grad_gain_one,
            grad_shift_one,
            grad_outward_off,
            grad_gain_two,
            grad_shift_two,
            grad_expand_off,
            grad_contract_off,
        )
    )
    return (
        output,
        grad_latents,
        grad_skip,
        sum_skipw,
        sum_skipb,
        sum_gain1,
        sum_shift1,
        sum_inward,
        sum_outward,
        sum_outb,
        sum_gain2,
        sum_shift2,
        sum_expand,
        sum_expandb,
        sum_contract,
        sum_contractb,
    )


def solution(mesh):
    wide, seq = mesh.shape["wide"], mesh.shape["seq"]
    devices = mesh.devices.reshape(wide // 4, 2, 2, seq)
    return jax.shard_map(
        per_device,
        mesh=Mesh(devices, WIDE + ("seq",)),
        in_specs=(
            P(WIDE, "seq", None),
            P(WIDE, None, "seq"),
            P(WIDE),
            P(WIDE, "seq", None),
            P("seq", None),
            P("seq"),
            P("seq"),
            P("seq"),
            P("seq", None),
            P("seq", None),
            P("seq"),
            P("seq"),
            P("seq"),
            P("seq", None),
            P("seq"),
            P("seq", None),
            P("seq"),
        ),
        out_specs=(
            P(WIDE, "seq", None),
            P(WIDE, "seq", None),
            P(WIDE, None, "seq"),
            P("seq", None),
            P("seq"),
            P("seq"),
            P("seq"),
            P("seq", None),
            P("seq", None),
            P("seq"),
            P("seq"),
            P("seq"),
            P("seq", None),
            P("seq"),
            P("seq", None),
            P("seq"),
        ),
        check_vma=False,
    )
```

```python
import jax
import jax.numpy as jnp
from jax import lax
from jax.experimental import pallas as pl
from jax.experimental.pallas import tpu as pltpu
from jax.sharding import Mesh
from jax.sharding import PartitionSpec as P

HEAD_DIM = 72

EPS = 1e-05
NEG = -1e30
WIDE = ("z", "x", "c")
BF16 = jnp.bfloat16
F32 = jnp.float32


def across(left_side, right_side):
    return lax.dot_general(
        left_side, right_side, (((0,), (0,)), ((), ())), preferred_element_type=F32
    )


def against(left_side, right_side):
    return lax.dot_general(
        left_side, right_side, (((1,), (1,)), ((), ())), preferred_element_type=F32
    )


def simple(left_side, right_side):
    return jnp.dot(left_side, right_side, preferred_element_type=F32)


def pick(array, index, size, axis=0):
    return lax.dynamic_slice_in_dim(array, index * size, size, axis)


def flip(array, axis):
    return lax.ppermute(array, axis, [(0, 1), (1, 0)])


def ordered(mine, other, index, axis=0):
    return jnp.where(
        index == 0,
        jnp.concatenate([mine, other], axis),
        jnp.concatenate([other, mine], axis),
    )


def fast_mesh():
    return lax.axis_size("seq") == 2 and lax.axis_size("z") == 4


def gather_weight(shard):
    if not fast_mesh():
        return lax.all_gather(shard, "seq", axis=0, tiled=True)
    place = lax.axis_index("x") * 2 + lax.axis_index("c")
    quarter = pick(shard, place, shard.shape[0] // 4)
    other = lax.all_gather(flip(quarter, "seq"), ("x", "c"), axis=0, tiled=True)
    return ordered(shard, other, lax.axis_index("seq"))


def swap(array, axis, step):
    ways = lax.axis_size(axis)
    return lax.ppermute(array, axis, [(i, i ^ step) for i in range(ways)])


def add(left, right):
    return (left.astype(F32) + right.astype(F32)).astype(BF16)


def block(array, index, axis):
    return lax.dynamic_index_in_dim(array, index, axis, keepdims=False)


def fold(blocks, axis):
    index = lax.axis_index(axis)
    return add(block(blocks, index, 0), flip(block(blocks, 1 - index, 0), axis))


def spread(part, axis):
    return ordered(part, flip(part, axis), lax.axis_index(axis))


def reduce_weight(grad, offload=False):
    if not fast_mesh():
        part = lax.psum_scatter(
            grad.astype(BF16), "seq", scatter_dimension=0, tiled=True
        )
        return lax.psum(part, WIDE).astype(F32)
    rows, columns = grad.shape
    core = lax.axis_index("c")
    blocks = grad.astype(BF16).reshape(2, 2, rows // 4, columns)
    chip = add(block(blocks, core, 1), flip(block(blocks, 1 - core, 1), "c"))
    part = fold(chip, "seq")
    if offload:
        part = lax.psum(part, ("z", "x"))
    else:
        part = fold(part.reshape(2, rows // 8, columns), "x")
        part = add(part, swap(part, "z", 1))
        part = add(part, swap(part, "z", 2))
        part = spread(part, "x")
    return spread(part, "c").astype(F32)


def gather_vectors(vectors):
    joined = jnp.concatenate(vectors)
    count = joined.shape[0]
    if fast_mesh():
        mine = joined.reshape(1, count)
        everything = ordered(mine, flip(mine, "seq"), lax.axis_index("seq"))
    else:
        everything = lax.all_gather(joined.reshape(1, count), "seq", axis=0, tiled=True)
    out, start = [], 0
    for vector in vectors:
        size = vector.shape[0]
        out.append(everything[:, start : start + size].reshape(-1).astype(F32))
        start += size
    return out


def reduce_vectors(vectors):
    ways = lax.axis_size("seq")
    side = lax.axis_index("seq")
    joined = jnp.concatenate(vectors)
    if fast_mesh():
        joined = jnp.concatenate([joined, jnp.zeros((-joined.shape[0]) % 16384, F32)])
        parts = lax.all_gather(joined.reshape(-1, 1024), WIDE + ("seq",), axis=0)
        total = jnp.sum(parts, 0).reshape(-1)
    else:
        total = lax.psum(joined, WIDE + ("seq",))
    out, start = [], 0
    for vector in vectors:
        size = vector.shape[0] // ways
        out.append(lax.dynamic_slice_in_dim(total, start + side * size, size, 0))
        start += vector.shape[0]
    return out


def share_items(array, per, axis):
    ways, side = lax.axis_size("seq"), lax.axis_index("seq")
    items, size = array.shape[0], array.shape[axis]
    array = jnp.pad(array, [(0, per * ways - items)] + [(0, 0)] * (array.ndim - 1))
    if ways == 2:
        return ordered(
            pick(array, side, per), flip(pick(array, 1 - side, per), "seq"), side, axis
        )
    shape = list(array.shape)
    shape[0], shape[axis] = per, size * ways
    whole = jnp.zeros(shape, array.dtype)
    for hop in range(ways):
        piece = pick(array, (side + hop) % ways, per)
        if hop:
            piece = lax.ppermute(
                piece, "seq", [(i, (i + hop) % ways) for i in range(ways)]
            )
        source = (side - hop) % ways
        whole = lax.dynamic_update_slice_in_dim(whole, piece, source * size, axis)
    return whole


def return_items(whole, items, axis):
    ways, side = lax.axis_size("seq"), lax.axis_index("seq")
    per, size = whole.shape[0], whole.shape[axis] // ways
    if ways == 2:
        mine = pick(whole, side, size, axis)
        other = flip(pick(whole, 1 - side, size, axis), "seq")
        return ordered(mine, other, side)[:items]
    shape = list(whole.shape)
    shape[0], shape[axis] = per * ways, size
    array = jnp.zeros(shape, whole.dtype)
    for hop in range(ways):
        piece = pick(whole, (side + hop) % ways, size, axis)
        if hop:
            piece = lax.ppermute(
                piece, "seq", [(i, (i + hop) % ways) for i in range(ways)]
            )
        source = (side - hop) % ways
        array = lax.dynamic_update_slice_in_dim(array, piece, source * per, 0)
    return array[:items]


def normalize(hidden):
    mean_val = jnp.mean(hidden, -1, keepdims=True)
    centred = hidden - mean_val
    scale = lax.rsqrt(jnp.mean(centred * centred, -1, keepdims=True) + EPS)
    return centred * scale, scale


def norm_back(grad, hidden, gain):
    xhat, scale = normalize(hidden)
    inner = grad * gain
    back = scale * (
        inner
        - jnp.mean(inner, -1, keepdims=True)
        - xhat * jnp.mean(inner * xhat, -1, keepdims=True)
    )
    return back, jnp.sum(grad * xhat, 0), jnp.sum(grad, 0)


LANES = 128


def head_window(head):
    start = head * HEAD_DIM
    first = start // LANES * LANES
    size = LANES if start + HEAD_DIM <= first + LANES else 2 * LANES
    return first, size, start - first


def head_mask(size, offset):
    lane = lax.broadcasted_iota(jnp.int32, (1, size), 1)
    return (lane >= offset) & (lane < offset + HEAD_DIM)


def head_groups(width, slots):
    heads = [(head,) + head_window(head) for head in range(width // HEAD_DIM)]
    count = max(1, 2048 // slots)
    return [heads[i : i + count] for i in range(0, len(heads), count)]


def masked(ref, first, size, offset):
    return jnp.where(head_mask(size, offset), ref[:, first : first + size], 0)


def place(ref, start, size, offset, result):
    result = result.astype(BF16)
    if offset:
        result = jnp.where(
            head_mask(size, offset), result, ref[:, start : start + size]
        )
    ref[:, start : start + size] = result


def attend_kernel(lengths, qkv, mixed, probs_out):
    slots, width = mixed.shape
    live = lax.broadcasted_iota(jnp.int32, (1, slots), 1) < lengths[pl.program_id(0)]
    for group in head_groups(width, slots):
        scores = [
            against(
                masked(qkv, first, size, offset),
                qkv[:, width + first : width + first + size],
            )
            for _, first, size, offset in group
        ]
        scores = [jnp.where(live, s * HEAD_DIM ** (-0.5), NEG) for s in scores]
        raised = [jnp.exp(s - jnp.max(s, -1, keepdims=True)) for s in scores]
        probs = [
            (r * (1.0 / jnp.sum(r, -1, keepdims=True))).astype(BF16) for r in raised
        ]
        results = [
            simple(p, qkv[:, 2 * width + first : 2 * width + first + size])
            for p, (_, first, size, _) in zip(probs, group)
        ]
        for p, result, (head, first, size, offset) in zip(probs, results, group):
            probs_out[head * slots : (head + 1) * slots, :] = p
            place(mixed, first, size, offset, result)


def attend(qkv, lengths):
    per = lengths.shape[0]
    rows, width = qkv.shape[0], qkv.shape[1] // 3
    slots, heads = rows // per, width // HEAD_DIM
    return pl.pallas_call(
        attend_kernel,
        out_shape=(
            jax.ShapeDtypeStruct((rows, width), BF16),
            jax.ShapeDtypeStruct((rows * heads, slots), BF16),
        ),
        grid_spec=pltpu.PrefetchScalarGridSpec(
            num_scalar_prefetch=1,
            grid=(per,),
            in_specs=[pl.BlockSpec((slots, 3 * width), lambda i, _: (i, 0))],
            out_specs=(
                pl.BlockSpec((slots, width), lambda i, _: (i, 0)),
                pl.BlockSpec((heads * slots, slots), lambda i, _: (i, 0)),
            ),
        ),
        compiler_params=pltpu.CompilerParams(vmem_limit_bytes=56 << 20),
        cost_estimate=pl.CostEstimate(
            flops=4 * rows * slots * width,
            transcendentals=rows * slots * heads,
            bytes_accessed=8 * rows * width + 2 * rows * heads * slots,
        ),
        name="attend",
    )(lengths, qkv)


def attend_back_kernel(qkv, probs_in, grad_mixed, grad_qkv):
    slots, width = grad_mixed.shape
    scale = HEAD_DIM ** (-0.5)
    for group in head_groups(width, slots):
        grads = [masked(grad_mixed, *window) for _, *window in group]
        grad_probs = [
            against(g, qkv[:, 2 * width + first : 2 * width + first + size])
            for g, (_, first, size, _) in zip(grads, group)
        ]
        probs = [
            probs_in[head * slots : (head + 1) * slots, :] for head, _, _, _ in group
        ]
        grad_values = [across(p, g) for p, g in zip(probs, grads)]
        probs = [p.astype(F32) for p in probs]
        sums = [
            jnp.sum(g * p, -1, keepdims=True) for g, p in zip(grad_probs, probs)
        ]
        scores = [
            (p * (g - total)).astype(BF16)
            for p, g, total in zip(probs, grad_probs, sums)
        ]
        grad_queries = [
            simple(s, qkv[:, width + first : width + first + size]) * scale
            for s, (_, first, size, _) in zip(scores, group)
        ]
        grad_keys = [
            across(s, qkv[:, first : first + size]) * scale
            for s, (_, first, size, _) in zip(scores, group)
        ]
        for part, results in enumerate((grad_queries, grad_keys, grad_values)):
            for result, (_, first, size, offset) in zip(results, group):
                place(grad_qkv, part * width + first, size, offset, result)


def attend_back(qkv, probs, grad_mixed, per):
    rows, width = grad_mixed.shape
    slots, heads = rows // per, width // HEAD_DIM
    return pl.pallas_call(
        attend_back_kernel,
        out_shape=jax.ShapeDtypeStruct((rows, 3 * width), BF16),
        grid=(per,),
        in_specs=[
            pl.BlockSpec((slots, 3 * width), lambda i: (i, 0)),
            pl.BlockSpec((heads * slots, slots), lambda i: (i, 0)),
            pl.BlockSpec((slots, width), lambda i: (i, 0)),
        ],
        out_specs=pl.BlockSpec((slots, 3 * width), lambda i: (i, 0)),
        compiler_params=pltpu.CompilerParams(vmem_limit_bytes=56 << 20),
        cost_estimate=pl.CostEstimate(
            flops=8 * rows * slots * width,
            transcendentals=0,
            bytes_accessed=14 * rows * width + 2 * rows * heads * slots,
        ),
        name="attend_back",
    )(qkv, probs, grad_mixed)


def gelu_pair(upper):
    below = 0.5 * (1.0 + lax.erf(upper * 0.7071067811865476))
    bell = jnp.exp(-0.5 * upper * upper) * 0.3989422804014327
    return (upper * below).astype(BF16), (below + upper * bell).astype(BF16)


def per_device(
    latents,
    skip_store,
    lengths,
    cotangent,
    skip_weight,
    skip_bias,
    first_gain,
    first_shift,
    inward_weight,
    outward_weight,
    outward_bias,
    second_gain,
    second_shift,
    expand_weight,
    expand_bias,
    contract_weight,
    contract_bias,
):
    items, slot_dev, width = latents.shape
    ways, side = lax.axis_size("seq"), lax.axis_index("seq")
    slots = slot_dev * ways
    per = -(-items // ways)
    rows = per * slots

    live = jnp.pad(lengths, (0, per * ways - items), constant_values=slots)
    live = pick(live, side, per)

    skip_rows = share_items(skip_store, per, 2)
    latent_rows = share_items(latents, per, 1)
    skip_matrix = gather_weight(skip_weight)
    (
        skip_offset,
        gain_first,
        shift_first,
        outward_offset,
        gain_second,
        shift_second,
        expand_offset,
        contract_offset,
    ) = gather_vectors(
        (
            skip_bias,
            first_gain,
            first_shift,
            outward_bias,
            second_gain,
            second_shift,
            expand_bias,
            contract_bias,
        )
    )
    inward_weight, skip_rows, latent_rows = lax.optimization_barrier(
        (inward_weight, skip_rows, latent_rows)
    )
    inward_matrix = gather_weight(inward_weight)
    outward_matrix = gather_weight(outward_weight)
    expand_matrix = gather_weight(expand_weight)
    contract_matrix = gather_weight(contract_weight)
    grad_out = share_items(cotangent, per, 1).reshape(rows, width)

    joined = jnp.concatenate([latent_rows, skip_rows], -1).reshape(rows, 2 * width)
    base = simple(joined, skip_matrix) + skip_offset
    first_normed = (normalize(base)[0] * gain_first + shift_first).astype(BF16)
    qkv_vals = simple(first_normed, inward_matrix).astype(BF16)
    mixed_rows, probs = attend(qkv_vals, live)
    middle = base + simple(mixed_rows, outward_matrix) + outward_offset
    second_normed = (normalize(middle)[0] * gain_second + shift_second).astype(BF16)
    upper = simple(second_normed, expand_matrix) + expand_offset
    activated, slope = lax.optimization_barrier(gelu_pair(upper))
    result = middle + simple(activated, contract_matrix) + contract_offset
    output = return_items(result.astype(BF16).reshape(per, slots, width), items, 1)

    sum_contract = reduce_weight(across(activated, grad_out), True)
    grad_result = grad_out.astype(F32)
    grad_contract_off = jnp.sum(grad_result, 0)
    grad_act = against(grad_out, contract_matrix)
    grad_upper = (grad_act * slope.astype(F32)).astype(BF16)
    sum_expand = reduce_weight(across(second_normed, grad_upper))
    grad_expand_off = jnp.sum(grad_upper.astype(F32), 0)
    grad_second = against(grad_upper, expand_matrix)
    grad_mid_ln, grad_gain_two, grad_shift_two = norm_back(
        grad_second, middle, gain_second
    )
    grad_middle = grad_result + grad_mid_ln
    grad_branch = grad_middle.astype(BF16)
    sum_outward = reduce_weight(across(mixed_rows, grad_branch))
    grad_outward_off = jnp.sum(grad_branch.astype(F32), 0)
    grad_mixed = against(grad_branch, outward_matrix).astype(BF16)
    grad_qkv = attend_back(qkv_vals, probs, grad_mixed, per)
    sum_inward = reduce_weight(across(first_normed, grad_qkv))
    grad_first = against(grad_qkv, inward_matrix)
    grad_base_ln, grad_gain_one, grad_shift_one = norm_back(
        grad_first, base, gain_first
    )
    grad_base = (grad_middle + grad_base_ln).astype(BF16)
    sum_skipw = reduce_weight(across(joined, grad_base))
    grad_skip_off = jnp.sum(grad_base.astype(F32), 0)
    grad_joined = against(grad_base, skip_matrix).astype(BF16)
    grad_joined = grad_joined.reshape(per, slots, 2 * width)
    grad_latents = return_items(grad_joined[:, :, :width], items, 1).astype(F32)
    grad_skip = return_items(grad_joined[:, :, width:], items, 2)
    (
        sum_skipb,
        sum_gain1,
        sum_shift1,
        sum_outb,
        sum_gain2,
        sum_shift2,
        sum_expandb,
        sum_contractb,
    ) = reduce_vectors(
        (
            grad_skip_off,
            grad_gain_one,
            grad_shift_one,
            grad_outward_off,
            grad_gain_two,
            grad_shift_two,
            grad_expand_off,
            grad_contract_off,
        )
    )
    return (
        output,
        grad_latents,
        grad_skip,
        sum_skipw,
        sum_skipb,
        sum_gain1,
        sum_shift1,
        sum_inward,
        sum_outward,
        sum_outb,
        sum_gain2,
        sum_shift2,
        sum_expand,
        sum_expandb,
        sum_contract,
        sum_contractb,
    )


def solution(mesh):
    wide, seq = mesh.shape["wide"], mesh.shape["seq"]
    devices = mesh.devices.reshape(wide // 4, 2, 2, seq)
    return jax.shard_map(
        per_device,
        mesh=Mesh(devices, WIDE + ("seq",)),
        in_specs=(
            P(WIDE, "seq", None),
            P(WIDE, None, "seq"),
            P(WIDE),
            P(WIDE, "seq", None),
            P("seq", None),
            P("seq"),
            P("seq"),
            P("seq"),
            P("seq", None),
            P("seq", None),
            P("seq"),
            P("seq"),
            P("seq"),
            P("seq", None),
            P("seq"),
            P("seq", None),
            P("seq"),
        ),
        out_specs=(
            P(WIDE, "seq", None),
            P(WIDE, "seq", None),
            P(WIDE, None, "seq"),
            P("seq", None),
            P("seq"),
            P("seq"),
            P("seq"),
            P("seq", None),
            P("seq", None),
            P("seq"),
            P("seq"),
            P("seq"),
            P("seq", None),
            P("seq"),
            P("seq", None),
            P("seq"),
        ),
        check_vma=False,
    )
```

```python
import functools

import jax
import jax.numpy as jnp
from jax import lax
from jax.experimental import pallas as pl
from jax.experimental.pallas import tpu as pltpu
from jax.sharding import Mesh
from jax.sharding import PartitionSpec as P

HEAD_DIM = 72
WIDTH = 16 * HEAD_DIM

EPS = 1e-05
NEG = -1e30
PLANE = ("z", "x", "c")
WIDE = ("w",) + PLANE
BF16 = jnp.bfloat16
F32 = jnp.float32
LANES = 128

def across(left_side, right_side):
    return lax.dot_general(
        left_side, right_side, (((0,), (0,)), ((), ())), preferred_element_type=F32
    )


def against(left_side, right_side):
    return lax.dot_general(
        left_side, right_side, (((1,), (1,)), ((), ())), preferred_element_type=F32
    )


def simple(left_side, right_side):
    return jnp.dot(left_side, right_side, preferred_element_type=F32)


def pick(array, index, size, axis=0):
    return lax.dynamic_slice_in_dim(array, index * size, size, axis)


def flip(array, axis):
    return lax.ppermute(array, axis, [(0, 1), (1, 0)])


def ordered(mine, other, index, axis=0):
    return jnp.where(
        index == 0,
        jnp.concatenate([mine, other], axis),
        jnp.concatenate([other, mine], axis),
    )


class Chain:
    def __init__(self):
        self.last = ()

    def enter(self, *values):
        values = lax.optimization_barrier(values + self.last)[: len(values)]
        return values

    def leave(self, *values):
        self.last = values[:1]
        return values if len(values) > 1 else values[0]

    def run(self, function, *values):
        out = function(*self.enter(*values))
        self.last = tuple(out)[:1] if isinstance(out, (tuple, list)) else (out,)
        return out


def fast_mesh():
    return lax.axis_size("seq") == 2 and lax.axis_size("w") == 2


def added(parts):
    if len(parts) == 1:
        return parts[0]
    return (parts[0].astype(F32) + parts[1].astype(F32)).astype(BF16)


def block(array, index, axis):
    return lax.dynamic_index_in_dim(array, index, axis, keepdims=False)


def eighth(shard):
    place = lax.axis_index("z") * 4 + lax.axis_index("x") * 2 + lax.axis_index("c")
    return pick(shard, place, shard.shape[0] // 8)


def share(piece):
    return lax.all_gather(piece, PLANE, axis=0, tiled=True)


class Reduction:
    def __init__(self, chain, name, lefts, rights):
        self.chain = chain
        if fast_mesh():
            core = lax.axis_index("c").reshape(1)
            count = len(lefts)
            sent, keep = chain.run(
                lambda *a: core_gradients(name, core, a[:count], a[count:]),
                *lefts,
                *rights,
            )
            shape = (2, 2, 2) + sent.shape[1:]
            self.parts = (keep.reshape(shape), flip(sent.reshape(shape), "c"))
            self.names = ["seq", "z", "x", "w", None]
        else:
            axis = int(len(rights) > 1)
            pairs = zip(lefts, rights) if axis else ((a, rights[0]) for a in lefts)
            grad = jnp.concatenate([across(*p).astype(BF16) for p in pairs], axis)
            part = lax.psum_scatter(grad, "seq", scatter_dimension=0, tiled=True)
            self.total, self.names = lax.psum(part, WIDE), []

    def step(self):
        if not self.names:
            return
        name = self.names.pop(0)
        parts = self.chain.enter(*self.parts)
        if name is None:
            self.total = share(self.chain.leave(added(parts)))
        elif name == "w":
            sent = self.chain.leave(added(parts))
            self.parts = (sent, flip(sent, name))
        else:
            index = lax.axis_index(name)
            sent = added([block(part, 1 - index, 0) for part in parts])
            keep = added([block(part, index, 0) for part in parts])
            sent, keep = self.chain.leave(sent, keep)
            self.parts = (keep, flip(sent, name))

    def finish(self):
        assert not self.names
        return self.chain.run(lambda a: a.astype(F32), self.total)


def gather_vectors(vectors):
    joined = jnp.concatenate(vectors)
    count = joined.shape[0]
    if fast_mesh():
        mine = joined.reshape(1, count)
        everything = ordered(mine, flip(mine, "seq"), lax.axis_index("seq"))
    else:
        everything = lax.all_gather(joined.reshape(1, count), "seq", axis=0, tiled=True)
    out, start = [], 0
    for vector in vectors:
        size = vector.shape[0]
        out.append(everything[:, start : start + size].reshape(-1).astype(F32))
        start += size
    return out


class VectorReduction:
    def __init__(self, chain, vectors):
        self.chain, self.sizes = chain, [vector.shape[1] for vector in vectors]
        self.total = chain.run(lambda *a: jnp.concatenate(a, 1), *vectors)
        self.names = ["seq", "c", "z", "x", "w"]
        if fast_mesh():
            self.got = flip(self.total, self.names.pop(0))
        else:
            self.total, self.names = lax.psum(self.total, WIDE + ("seq",)), []

    def step(self):
        if fast_mesh():
            self.total = self.chain.run(jnp.add, self.total, self.got)
            if self.names:
                self.got = flip(self.total, self.names.pop(0))

    def finish(self):
        assert not self.names
        ways, side = lax.axis_size("seq"), lax.axis_index("seq")
        out, start = [], 0
        for whole in self.sizes:
            size = whole // ways
            shards = self.total[:, start : start + whole].reshape(ways, size)
            out.append(block(shards, side, 0))
            start += whole
        return out


def start_items(array, per):
    ways, side = lax.axis_size("seq"), lax.axis_index("seq")
    padding = [(0, per * ways - array.shape[0])] + [(0, 0)] * (array.ndim - 1)
    array = jnp.pad(array, padding)
    pieces = [pick(array, side, per)]
    for hop in range(1, ways):
        piece = pick(array, (side + hop) % ways, per)
        pieces.append(
            lax.ppermute(piece, "seq", [(i, (i + hop) % ways) for i in range(ways)])
        )
    return tuple(pieces)


def joined_pieces(pieces, axis):
    ways, side = lax.axis_size("seq"), lax.axis_index("seq")
    if ways == 2:
        return ordered(pieces[0], pieces[1], side, axis)
    size = pieces[0].shape[axis]
    shape = list(pieces[0].shape)
    shape[axis] = size * ways
    whole = jnp.zeros(shape, pieces[0].dtype)
    for hop, piece in enumerate(pieces):
        source = (side - hop) % ways
        whole = lax.dynamic_update_slice_in_dim(whole, piece, source * size, axis)
    return whole


def return_items(whole, axis):
    ways, side = lax.axis_size("seq"), lax.axis_index("seq")
    size = whole.shape[axis] // ways
    pieces = [pick(whole, side, size, axis)]
    for hop in range(1, ways):
        piece = pick(whole, (side + hop) % ways, size, axis)
        pieces.append(
            lax.ppermute(piece, "seq", [(i, (i + hop) % ways) for i in range(ways)])
        )
    return tuple(pieces)


HINT = pl.CostEstimate(flops=10**13, transcendentals=0, bytes_accessed=10**9)


def block_loader(parts, offset, blocks, side, sems):
    count, size, _ = blocks.shape
    rows, columns = parts[0].shape
    first = pl.program_id(0) == 0
    copies = []
    for b in range(count):
        copies.append([])
        if len(parts) == 1:
            row, column = divmod(b, columns // size)
            source = parts[0].at[pl.ds(row * size, size), pl.ds(column * size, size)]
            copy = pltpu.make_async_copy(source, blocks.at[b], sems.at[0, b])
            copies[b].append((first, copy))
        elif rows >= size:
            half, place = divmod(b, rows // size)
            for p, part in enumerate(parts):
                mine = side == half if p == 0 else side != half
                source = part.at[pl.ds(place * size, size), :]
                copy = pltpu.make_async_copy(source, blocks.at[b], sems.at[0, b])
                copies[b].append((jnp.logical_and(first, mine), copy))
        else:
            for p, part in enumerate(parts):
                start = pl.multiple_of((side if p == 0 else 1 - side) * rows, 16)
                column = (b + (offset if p else 0)) * size
                copy = pltpu.make_async_copy(
                    part.at[:, pl.ds(column, size)],
                    blocks.at[b, pl.ds(start, rows), :],
                    sems.at[p, b],
                )
                copies[b].append((first, copy))
    for pair in copies:
        for when, copy in pair:
            pl.when(when)(copy.start)

    def wait(b):
        for when, copy in copies[b]:
            pl.when(when)(copy.wait)

    return wait


def dense(name, body, rows_in, vectors, weight, outs, sums=(), steps=2):
    rows = rows_in[0].shape[0]
    tile = rows // steps
    count, offset, parts = weight
    cuts = [len(rows_in), len(vectors), len(parts), len(outs), len(sums)]

    def kernel(side, *refs):
        groups = []
        for size in cuts:
            groups.append(refs[:size])
            refs = refs[size:]
        blocks, sems = refs
        wait = block_loader(groups[2], offset, blocks, side[0], sems)
        if sums:

            @pl.when(pl.program_id(0) == 0)
            def _():
                for ref in groups[4]:
                    ref[...] = jnp.zeros_like(ref)

        body(wait, blocks, groups[0], groups[1], groups[3], groups[4])

    return pl.pallas_call(
        kernel,
        out_shape=tuple(jax.ShapeDtypeStruct((rows, c), d) for c, d in outs)
        + tuple(jax.ShapeDtypeStruct((1, c), F32) for c in sums),
        grid_spec=pltpu.PrefetchScalarGridSpec(
            num_scalar_prefetch=1,
            grid=(steps,),
            in_specs=[
                pl.BlockSpec((tile, a.shape[1]), lambda i, _: (i, 0)) for a in rows_in
            ]
            + [pl.BlockSpec(a.shape, lambda i, _: (0, 0)) for a in vectors]
            + [pl.BlockSpec(memory_space=pl.ANY) for _ in parts],
            out_specs=tuple(pl.BlockSpec((tile, c), lambda i, _: (i, 0)) for c, _ in outs)
            + tuple(pl.BlockSpec((1, c), lambda i, _: (0, 0)) for c in sums),
            scratch_shapes=[
                pltpu.VMEM((count, WIDTH, WIDTH), BF16),
                pltpu.SemaphoreType.DMA((2, count)),
            ],
        ),
        compiler_params=pltpu.CompilerParams(vmem_limit_bytes=60 << 20),
        cost_estimate=HINT,
        name=name,
    )(lax.axis_index("seq").reshape(1), *rows_in, *vectors, *parts)


def normalize(hidden):
    mean_val = jnp.mean(hidden, -1, keepdims=True)
    centred = hidden - mean_val
    scale = lax.rsqrt(jnp.mean(centred * centred, -1, keepdims=True) + EPS)
    return centred * scale, scale


def add_sum(ref, values):
    ref[...] += jnp.sum(values, 0, keepdims=True)


def columns_of(b):
    return slice(b * WIDTH, (b + 1) * WIDTH)


def base_body(wait, blocks, rows, vectors, outs, sums):
    wait(0)
    total = simple(rows[0][...], blocks[0])
    wait(1)
    total = total + simple(rows[1][...], blocks[1]) + vectors[0][...]
    outs[0][...] = total
    outs[1][...] = (normalize(total)[0] * vectors[1][...] + vectors[2][...]).astype(
        BF16
    )


def wide_body(wait, blocks, rows, vectors, outs, sums):
    for b in range(blocks.shape[0]):
        wait(b)
        outs[0][:, columns_of(b)] = simple(rows[0][...], blocks[b]).astype(BF16)


def middle_body(wait, blocks, rows, vectors, outs, sums):
    wait(0)
    total = simple(rows[0][...], blocks[0]) + rows[1][...] + vectors[0][...]
    outs[0][...] = total
    outs[1][...] = (normalize(total)[0] * vectors[1][...] + vectors[2][...]).astype(
        BF16
    )


def expand_body(wait, blocks, rows, vectors, outs, sums):
    for b in range(blocks.shape[0]):
        wait(b)
        upper = simple(rows[0][...], blocks[b]) + vectors[0][:, columns_of(b)]
        below = 0.5 * (1.0 + lax.erf(upper * 0.7071067811865476))
        bell = jnp.exp(-0.5 * upper * upper) * 0.3989422804014327
        outs[0][:, columns_of(b)] = (upper * below).astype(BF16)
        outs[1][:, columns_of(b)] = (below + upper * bell).astype(BF16)


def contract_body(wait, blocks, rows, vectors, outs, sums):
    total = rows[1][...] + vectors[0][...]
    for b in range(blocks.shape[0]):
        wait(b)
        total = total + simple(rows[0][:, columns_of(b)], blocks[b])
    outs[0][...] = total.astype(BF16)


def upper_back_body(wait, blocks, rows, vectors, outs, sums):
    grad = rows[0][...]
    add_sum(sums[1], grad.astype(F32))
    for b in range(blocks.shape[0]):
        wait(b)
        upper = against(grad, blocks[b]) * rows[1][:, columns_of(b)].astype(F32)
        upper = upper.astype(BF16)
        outs[0][:, columns_of(b)] = upper
        add_sum(sums[0].at[:, columns_of(b)], upper.astype(F32))


def norm_back_body(wait, blocks, rows, vectors, outs, sums):
    grad = None
    for b in range(blocks.shape[0]):
        wait(b)
        part = against(rows[0][:, columns_of(b)], blocks[b])
        grad = part if grad is None else grad + part
    xhat, scale = normalize(rows[1][...])
    inner = grad * vectors[0][...]
    back = scale * (
        inner
        - jnp.mean(inner, -1, keepdims=True)
        - xhat * jnp.mean(inner * xhat, -1, keepdims=True)
    )
    total = rows[2][...].astype(F32) + back
    rounded = total.astype(BF16)
    outs[0][...] = rounded
    if len(outs) > 1:
        outs[1][...] = total
    add_sum(sums[0], grad * xhat)
    add_sum(sums[1], grad)
    add_sum(sums[2], rounded.astype(F32))


def against_body(wait, blocks, rows, vectors, outs, sums):
    for b in range(blocks.shape[0]):
        wait(b)
        result = against(rows[0][...], blocks[b]).astype(BF16)
        size = outs[b].shape[1]
        outs[b][...] = result[:, :size]
        if size < WIDTH:
            outs[b + 1][...] = result[:, size:]


def core_gradients(name, core, lefts, rights):
    rows = rights[0].shape[0]
    columns = sum(right.shape[1] for right in rights)
    stacked = len(rights) == 1
    depth = sum(left.shape[1] for left in lefts) if stacked else WIDTH
    tiles, unit = depth // WIDTH, depth // 16
    per = WIDTH // unit // 2
    count = len(lefts)
    ends = [0]
    for array in lefts if stacked else rights:
        ends.append(ends[-1] + array.shape[1] // WIDTH)

    def kernel(core_ref, *refs):
        left, right = refs[:count], refs[count : count + len(rights)]
        sent, keep = refs[count + len(rights) :]

        def run(left_ref, right_ref):
            grad = across(left_ref[...], right_ref[...]).astype(BF16)
            for mine in range(2):

                @pl.when(core_ref[0] == mine)
                def _():
                    for j in range(per):
                        own, other = 2 * j + mine, 2 * j + 1 - mine
                        keep[j] = grad[own * unit : (own + 1) * unit]
                        sent[j] = grad[other * unit : (other + 1) * unit]

        if count == 1:
            run(left[0], right[0])
        else:
            place = pl.program_id(0 if stacked else 1)
            for k in range(count):
                here = jnp.logical_and(place >= ends[k], place < ends[k + 1])
                pl.when(here)(
                    functools.partial(run, left[k], right[0 if stacked else k])
                )

    def clipped(index, k, blocks):
        return jnp.clip(index - ends[k], 0, blocks - 1)

    def left_spec(k, left):
        blocks = left.shape[1] // WIDTH
        if stacked:
            return pl.BlockSpec(
                (rows, WIDTH), lambda i, n, _: (0, clipped(i, k, blocks))
            )
        return pl.BlockSpec((rows, WIDTH), lambda i, n, _: (0, 0))

    def right_spec(k, right):
        blocks = right.shape[1] // WIDTH
        if stacked:
            return pl.BlockSpec((rows, WIDTH), lambda i, n, _: (0, n))
        return pl.BlockSpec((rows, WIDTH), lambda i, n, _: (0, clipped(n, k, blocks)))

    half = jax.ShapeDtypeStruct((8, unit, columns), BF16)
    return pl.pallas_call(
        kernel,
        out_shape=(half, half),
        grid_spec=pltpu.PrefetchScalarGridSpec(
            num_scalar_prefetch=1,
            grid=(tiles, columns // WIDTH),
            in_specs=[left_spec(k, left) for k, left in enumerate(lefts)]
            + [right_spec(k, right) for k, right in enumerate(rights)],
            out_specs=(pl.BlockSpec((per, unit, WIDTH), lambda i, n, _: (i, 0, n)),) * 2,
        ),
        compiler_params=pltpu.CompilerParams(vmem_limit_bytes=60 << 20),
        cost_estimate=HINT,
        name=name,
    )(core, *lefts, *rights)


def head_window(head):
    start = head * HEAD_DIM
    first = start // LANES * LANES
    size = LANES if start + HEAD_DIM <= first + LANES else 2 * LANES
    return first, size, start - first


def head_mask(size, offset):
    lane = lax.broadcasted_iota(jnp.int32, (1, size), 1)
    return (lane >= offset) & (lane < offset + HEAD_DIM)


def head_groups(width, slots):
    heads = [(head,) + head_window(head) for head in range(width // HEAD_DIM)]
    count = max(1, 2048 // slots)
    return [heads[i : i + count] for i in range(0, len(heads), count)]


def masked(ref, first, size, offset):
    return jnp.where(head_mask(size, offset), ref[:, first : first + size], 0)


def place(ref, start, size, offset, result):
    result = result.astype(BF16)
    if offset:
        result = jnp.where(
            head_mask(size, offset), result, ref[:, start : start + size]
        )
    ref[:, start : start + size] = result


def attend_kernel(lengths, qkv, mixed, probs_out):
    slots, width = mixed.shape
    live = lax.broadcasted_iota(jnp.int32, (1, slots), 1) < lengths[pl.program_id(0)]
    for group in head_groups(width, slots):
        scores = [
            against(
                masked(qkv, first, size, offset),
                qkv[:, width + first : width + first + size],
            )
            for _, first, size, offset in group
        ]
        scores = [jnp.where(live, s * HEAD_DIM ** (-0.5), NEG) for s in scores]
        raised = [jnp.exp(s - jnp.max(s, -1, keepdims=True)) for s in scores]
        probs = [
            (r * (1.0 / jnp.sum(r, -1, keepdims=True))).astype(BF16) for r in raised
        ]
        results = [
            simple(p, qkv[:, 2 * width + first : 2 * width + first + size])
            for p, (_, first, size, _) in zip(probs, group)
        ]
        for p, result, (head, first, size, offset) in zip(probs, results, group):
            probs_out[head * slots : (head + 1) * slots, :] = p
            place(mixed, first, size, offset, result)


def attend(qkv, lengths):
    per = lengths.shape[0]
    rows, width = qkv.shape[0], qkv.shape[1] // 3
    slots, heads = rows // per, width // HEAD_DIM
    return pl.pallas_call(
        attend_kernel,
        out_shape=(
            jax.ShapeDtypeStruct((rows, width), BF16),
            jax.ShapeDtypeStruct((rows * heads, slots), BF16),
        ),
        grid_spec=pltpu.PrefetchScalarGridSpec(
            num_scalar_prefetch=1,
            grid=(per,),
            in_specs=[pl.BlockSpec((slots, 3 * width), lambda i, _: (i, 0))],
            out_specs=(
                pl.BlockSpec((slots, width), lambda i, _: (i, 0)),
                pl.BlockSpec((heads * slots, slots), lambda i, _: (i, 0)),
            ),
        ),
        compiler_params=pltpu.CompilerParams(vmem_limit_bytes=56 << 20),
        cost_estimate=HINT,
        name="attend",
    )(lengths, qkv)


def attend_back_kernel(qkv, probs_in, grad_mixed, grad_qkv):
    slots, width = grad_mixed.shape
    scale = HEAD_DIM ** (-0.5)
    for group in head_groups(width, slots):
        grads = [masked(grad_mixed, *window) for _, *window in group]
        grad_probs = [
            against(g, qkv[:, 2 * width + first : 2 * width + first + size])
            for g, (_, first, size, _) in zip(grads, group)
        ]
        probs = [
            probs_in[head * slots : (head + 1) * slots, :] for head, _, _, _ in group
        ]
        grad_values = [across(p, g) for p, g in zip(probs, grads)]
        probs = [p.astype(F32) for p in probs]
        sums = [
            jnp.sum(g * p, -1, keepdims=True) for g, p in zip(grad_probs, probs)
        ]
        scores = [
            (p * (g - total)).astype(BF16)
            for p, g, total in zip(probs, grad_probs, sums)
        ]
        grad_queries = [
            simple(s, qkv[:, width + first : width + first + size]) * scale
            for s, (_, first, size, _) in zip(scores, group)
        ]
        grad_keys = [
            across(s, qkv[:, first : first + size]) * scale
            for s, (_, first, size, _) in zip(scores, group)
        ]
        for part, results in enumerate((grad_queries, grad_keys, grad_values)):
            for result, (_, first, size, offset) in zip(results, group):
                place(grad_qkv, part * width + first, size, offset, result)


def attend_back(qkv, probs, grad_mixed, per):
    rows, width = grad_mixed.shape
    slots, heads = rows // per, width // HEAD_DIM
    return pl.pallas_call(
        attend_back_kernel,
        out_shape=jax.ShapeDtypeStruct((rows, 3 * width), BF16),
        grid=(per,),
        in_specs=[
            pl.BlockSpec((slots, 3 * width), lambda i: (i, 0)),
            pl.BlockSpec((heads * slots, slots), lambda i: (i, 0)),
            pl.BlockSpec((slots, width), lambda i: (i, 0)),
        ],
        out_specs=pl.BlockSpec((slots, 3 * width), lambda i: (i, 0)),
        compiler_params=pltpu.CompilerParams(vmem_limit_bytes=56 << 20),
        cost_estimate=HINT,
        name="attend_back",
    )(qkv, probs, grad_mixed)


def per_device(
    latents,
    skip_store,
    lengths,
    cotangent,
    skip_weight,
    skip_bias,
    first_gain,
    first_shift,
    inward_weight,
    outward_weight,
    outward_bias,
    second_gain,
    second_shift,
    expand_weight,
    expand_bias,
    contract_weight,
    contract_bias,
):
    items, slot_dev, width = latents.shape
    ways, side = lax.axis_size("seq"), lax.axis_index("seq")
    slots = slot_dev * ways
    per = -(-items // ways)
    rows = per * slots
    fast = fast_mesh()
    chain = Chain()

    live = jnp.pad(lengths, (0, per * ways - items), constant_values=slots)
    live = pick(live, side, per)

    (
        skip_offset,
        gain_first,
        shift_first,
        outward_offset,
        gain_second,
        shift_second,
        expand_offset,
        contract_offset,
    ) = (
        vector.reshape(1, -1)
        for vector in gather_vectors(
            (
                skip_bias,
                first_gain,
                first_shift,
                outward_bias,
                second_gain,
                second_shift,
                expand_bias,
                contract_bias,
            )
        )
    )
    if fast:
        skip_piece = flip(chain.run(eighth, skip_weight), "seq")
        skip_parts = (skip_weight, share(skip_piece))
        attention_piece = flip(
            chain.run(
                lambda a, b: jnp.concatenate([eighth(a), eighth(b)], 1),
                inward_weight,
                outward_weight,
            ),
            "seq",
        )
        attention_other = share(attention_piece)
        inward_parts = (inward_weight, attention_other)
        outward_parts = (outward_weight, attention_other)
        skip_pieces = chain.run(lambda a: start_items(a, per), skip_store)
        latent_pieces = chain.run(lambda a: start_items(a, per), latents)
        skip_rows, latent_rows = chain.run(
            lambda a, b: (
                joined_pieces(a, 2).reshape(rows, width),
                joined_pieces(b, 1).reshape(rows, width),
            ),
            skip_pieces,
            latent_pieces,
        )
        expand_piece = flip(chain.run(eighth, expand_weight), "seq")
        contract_piece = flip(chain.run(eighth, contract_weight), "seq")
        grad_pieces = chain.run(lambda a: start_items(a, per), cotangent)
    else:
        skip_parts, inward_parts, outward_parts, expand_parts, contract_parts = (
            (lax.all_gather(shard, "seq", axis=0, tiled=True),)
            for shard in (
                skip_weight,
                inward_weight,
                outward_weight,
                expand_weight,
                contract_weight,
            )
        )
        skip_rows = joined_pieces(start_items(skip_store, per), 2)
        latent_rows = joined_pieces(start_items(latents, per), 1)
        grad_pieces = start_items(cotangent, per)
    skip_matrix, inward_matrix = (2, 0, skip_parts), (3, 0, inward_parts)
    outward_matrix = (1, 3, outward_parts)
    skip_rows, latent_rows = (a.reshape(rows, width) for a in (skip_rows, latent_rows))
    one, both = [(width, BF16)], [(width, F32), (width, BF16)]

    base, first_normed = chain.run(
        lambda a, b, *w: dense(
            "base",
            base_body,
            (a, b),
            (skip_offset, gain_first, shift_first),
            (2, 0, w),
            both,
        ),
        latent_rows,
        skip_rows,
        *skip_parts,
    )
    if fast:
        expand_parts = (expand_weight, share(*chain.enter(expand_piece)))
    (qkv_vals,) = chain.run(
        lambda a: dense("inward", wide_body, (a,), (), inward_matrix, [(3 * width, BF16)]),
        first_normed,
    )
    if fast:
        contract_parts = (contract_weight, share(*chain.enter(contract_piece)))
    expand_matrix, contract_matrix = (4, 0, expand_parts), (4, 0, contract_parts)
    mixed_rows, probs = chain.run(lambda a: attend(a, live), qkv_vals)
    middle, second_normed = dense(
        "middle",
        middle_body,
        (mixed_rows, base),
        (outward_offset, gain_second, shift_second),
        outward_matrix,
        both,
    )
    activated, slope = dense(
        "expand",
        expand_body,
        (second_normed,),
        (expand_offset,),
        expand_matrix,
        [(expand_offset.shape[1], BF16)] * 2,
    )
    chain.leave(activated)
    grad_out = chain.run(
        lambda *a: joined_pieces(a, 1).reshape(rows, width), *grad_pieces
    )
    contract_sum = Reduction(chain, "contract_grad", (activated,), (grad_out,))
    grad_upper, grad_expand_off, grad_contract_off = chain.run(
        lambda *a: dense(
            "upper_back",
            upper_back_body,
            a,
            (),
            contract_matrix,
            [(expand_offset.shape[1], BF16)],
            [expand_offset.shape[1], width],
        ),
        grad_out,
        slope,
    )
    contract_sum.step()
    expand_sum = Reduction(chain, "expand_grad", (second_normed,), (grad_upper,))
    grad_branch, grad_middle, grad_gain_two, grad_shift_two, grad_outward_off = chain.run(
        lambda *a: dense(
            "middle_back",
            norm_back_body,
            a,
            (gain_second,),
            expand_matrix,
            both[::-1],
            [width] * 3,
        ),
        grad_upper,
        middle,
        grad_out,
    )
    expand_sum.step()
    (grad_mixed,) = chain.run(
        lambda a: dense("mixed_back", against_body, (a,), (), outward_matrix, one),
        grad_branch,
    )
    grad_qkv = attend_back(qkv_vals, probs, grad_mixed, per)
    chain.leave(grad_qkv)
    contract_sum.step()
    attention_sum = Reduction(
        chain,
        "attention_grad",
        (first_normed, mixed_rows),
        (grad_qkv, grad_branch),
    )
    grad_base, grad_gain_one, grad_shift_one, grad_skip_off = chain.run(
        lambda *a: dense(
            "base_back", norm_back_body, a, (gain_first,), inward_matrix, one, [width] * 3
        ),
        grad_qkv,
        base,
        grad_middle,
    )
    vector_sum = VectorReduction(
        chain,
        (
            grad_skip_off,
            grad_gain_one,
            grad_shift_one,
            grad_outward_off,
            grad_gain_two,
            grad_shift_two,
            grad_expand_off,
            grad_contract_off,
        ),
    )
    attention_sum.step()
    contract_sum.step()
    expand_sum.step()
    skip_sum = Reduction(chain, "skip_grad", (latent_rows, skip_rows), (grad_base,))
    contract_sum.step()
    vector_sum.step()
    halves = ways == 2
    columns = [width] + ([width // 2] * 2 if halves else [width])
    grad_latents, *grad_skip = chain.run(
        lambda a: dense(
            "joined_back",
            against_body,
            (a,),
            (),
            skip_matrix,
            [(size, BF16) for size in columns],
        ),
        grad_base,
    )
    skip_sum.step()
    contract_sum.step()
    expand_sum.step()
    vector_sum.step()
    latent_pieces = chain.run(
        lambda a: return_items(a.reshape(per, slots, width), 1), grad_latents
    )
    if halves:
        skip_pieces = chain.run(
            lambda a, b: (jnp.where(side == 0, a, b), jnp.where(side == 0, b, a)),
            *grad_skip,
        )
        skip_pieces = [a.reshape(per, slots, width // 2) for a in skip_pieces]
        skip_pieces[1] = flip(skip_pieces[1], "seq")
    else:
        skip_pieces = return_items(grad_skip[0].reshape(per, slots, width), 2)
    (result,) = chain.run(
        lambda *a: dense(
            "contract", contract_body, a, (contract_offset,), contract_matrix, one
        ),
        activated,
        middle,
    )
    expand_sum.step()
    output_pieces = chain.run(
        lambda a: return_items(a.reshape(per, slots, width), 1), result
    )
    attention_sum.step()
    vector_sum.step()
    expand_sum.step()
    vector_sum.step()
    skip_sum.step()
    sum_contract = contract_sum.finish()
    attention_sum.step()
    vector_sum.step()
    attention_sum.step()
    skip_sum.step()
    skip_sum.step()
    attention_sum.step()
    skip_sum.step()
    sum_expand = expand_sum.finish()
    grad_latents = chain.run(
        lambda *a: joined_pieces(a, 0)[:items].astype(F32), *latent_pieces
    )
    grad_skip = chain.run(lambda *a: joined_pieces(a, 0)[:items], *skip_pieces)
    output = chain.run(lambda *a: joined_pieces(a, 0)[:items], *output_pieces)
    sum_attention = attention_sum.finish()
    sum_inward, sum_outward = jnp.split(sum_attention, [3 * width], 1)
    sum_skipw = skip_sum.finish()
    (
        sum_skipb,
        sum_gain1,
        sum_shift1,
        sum_outb,
        sum_gain2,
        sum_shift2,
        sum_expandb,
        sum_contractb,
    ) = vector_sum.finish()
    return (
        output,
        grad_latents,
        grad_skip,
        sum_skipw,
        sum_skipb,
        sum_gain1,
        sum_shift1,
        sum_inward,
        sum_outward,
        sum_outb,
        sum_gain2,
        sum_shift2,
        sum_expand,
        sum_expandb,
        sum_contract,
        sum_contractb,
    )


def solution(mesh):
    wide, seq = mesh.shape["wide"], mesh.shape["seq"]
    devices = mesh.devices.reshape(wide // 8, 2, 2, 2, seq)
    return jax.shard_map(
        per_device,
        mesh=Mesh(devices, WIDE + ("seq",)),
        in_specs=(
            P(WIDE, "seq", None),
            P(WIDE, None, "seq"),
            P(WIDE),
            P(WIDE, "seq", None),
            P("seq", None),
            P("seq"),
            P("seq"),
            P("seq"),
            P("seq", None),
            P("seq", None),
            P("seq"),
            P("seq"),
            P("seq"),
            P("seq", None),
            P("seq"),
            P("seq", None),
            P("seq"),
        ),
        out_specs=(
            P(WIDE, "seq", None),
            P(WIDE, "seq", None),
            P(WIDE, None, "seq"),
            P("seq", None),
            P("seq"),
            P("seq"),
            P("seq"),
            P("seq", None),
            P("seq", None),
            P("seq"),
            P("seq"),
            P("seq"),
            P("seq", None),
            P("seq"),
            P("seq", None),
            P("seq"),
        ),
        check_vma=False,
    )
```

```python
import functools

import jax
import jax.numpy as jnp
from jax import lax
from jax.experimental import pallas as pl
from jax.experimental.pallas import tpu as pltpu
from jax.sharding import Mesh
from jax.sharding import PartitionSpec as P

HEAD_DIM = 72
WIDTH = 16 * HEAD_DIM

EPS = 1e-05
NEG = -1e30
PLANE = ("z", "x", "c")
WIDE = ("w",) + PLANE
BF16 = jnp.bfloat16
F32 = jnp.float32
LANES = 128

def across(left_side, right_side):
    return lax.dot_general(
        left_side, right_side, (((0,), (0,)), ((), ())), preferred_element_type=F32
    )


def against(left_side, right_side):
    return lax.dot_general(
        left_side, right_side, (((1,), (1,)), ((), ())), preferred_element_type=F32
    )


def simple(left_side, right_side):
    return jnp.dot(left_side, right_side, preferred_element_type=F32)


def pick(array, index, size, axis=0):
    return lax.dynamic_slice_in_dim(array, index * size, size, axis)


def flip(array, axis):
    return lax.ppermute(array, axis, [(0, 1), (1, 0)])


def ordered(mine, other, index, axis=0):
    return jnp.where(
        index == 0,
        jnp.concatenate([mine, other], axis),
        jnp.concatenate([other, mine], axis),
    )


class Chain:
    def __init__(self):
        self.last = ()

    def enter(self, *values):
        values = lax.optimization_barrier(values + self.last)[: len(values)]
        return values

    def leave(self, *values):
        self.last = values[:1]
        return values if len(values) > 1 else values[0]

    def run(self, function, *values):
        out = function(*self.enter(*values))
        self.last = tuple(out)[:1] if isinstance(out, (tuple, list)) else (out,)
        return out


def fast_mesh():
    return lax.axis_size("seq") == 2 and lax.axis_size("w") == 2


def block(array, index, axis):
    return lax.dynamic_index_in_dim(array, index, axis, keepdims=False)


def eighth(shard):
    place = lax.axis_index("z") * 4 + lax.axis_index("x") * 2 + lax.axis_index("c")
    return pick(shard, place, shard.shape[0] // 8)


def share(piece):
    return lax.all_gather(piece, PLANE, axis=0, tiled=True)


class Reduction:
    def __init__(self, chain, name, lefts, rights, lanes=1):
        self.chain, self.lanes = chain, lanes
        self.cuts = [right.shape[1] for right in rights]
        if fast_mesh():
            core = lax.axis_index("c").reshape(1)
            count = len(lefts)
            sent, keep = chain.run(
                lambda *a: core_gradients(name, core, a[:count], a[count:]),
                *lefts,
                *rights,
            )
            self.parts = [(keep, flip(sent, "c"))] * lanes
            self.names = [["seq", "x", "z", "w"] for _ in range(lanes)]
        else:
            axis = int(len(rights) > 1)
            pairs = zip(lefts, rights) if axis else ((a, rights[0]) for a in lefts)
            grad = jnp.concatenate([across(*p).astype(BF16) for p in pairs], axis)
            part = lax.psum_scatter(grad, "seq", scatter_dimension=0, tiled=True)
            self.total, self.names = lax.psum(part, WIDE), None

    def step(self, lane=0):
        if self.names is None:
            return
        if not self.names[lane]:
            self.join()
            return
        name, parts = self.names[lane].pop(0), self.parts[lane]
        if name == "w":
            sent = self.chain.run(
                lambda *a: add(*(part.reshape(part.shape[1:]) for part in a)), *parts
            )
            self.parts[lane] = (sent, flip(sent, name))
        else:
            outer = 2 if name == "x" else 1
            lanes = self.lanes if name == "seq" else 1
            sent, keep = self.chain.run(
                functools.partial(fold, name, outer, lane if lanes > 1 else 0, lanes),
                *parts,
            )
            self.parts[lane] = (keep, flip(sent, name))

    def join(self):
        if self.names is None:
            return
        assert not any(self.names)
        parts = [part for pair in self.parts for part in pair]
        self.total = share(self.chain.run(add, *parts))

    def finish(self):
        return self.chain.run(functools.partial(widen, self.cuts), self.total)


def gather_vectors(chain, vectors):
    joined = chain.run(lambda *a: jnp.concatenate(a), *vectors)
    mine = joined.reshape(1, -1)
    if fast_mesh():
        everything = ordered(mine, flip(mine, "seq"), lax.axis_index("seq"))
    else:
        everything = lax.all_gather(mine, "seq", axis=0, tiled=True)
    out, start = [], 0
    for vector in vectors:
        size = vector.shape[0]
        out.append(everything[:, start : start + size].reshape(1, -1).astype(F32))
        start += size
    return out


class VectorReduction:
    def __init__(self, chain, vectors):
        self.chain, self.sizes = chain, [vector.shape[1] for vector in vectors]
        self.total = chain.run(lambda *a: jnp.concatenate(a, 1), *vectors)
        self.names = ["c", "x", "z", "w", "seq"]
        if fast_mesh():
            self.got = flip(self.total, self.names.pop(0))
        else:
            self.total, self.names = lax.psum(self.total, WIDE + ("seq",)), []

    def step(self):
        if fast_mesh():
            self.total = self.chain.run(add, self.total, self.got)
            if self.names:
                self.got = flip(self.total, self.names.pop(0))

    def finish(self):
        assert not self.names
        ways, side = lax.axis_size("seq"), lax.axis_index("seq")
        out, start = [], 0
        for whole in self.sizes:
            size = whole // ways
            shards = self.total[:, start : start + whole].reshape(ways, size)
            out.append(block(shards, side, 0))
            start += whole
        return out


def split_items(array, per):
    ways, side = lax.axis_size("seq"), lax.axis_index("seq")
    padding = [(0, per * ways - array.shape[0])] + [(0, 0)] * (array.ndim - 1)
    array = jnp.pad(array, padding)
    return tuple(pick(array, (side + hop) % ways, per) for hop in range(ways))


def split_parts(whole, axis):
    ways, side = lax.axis_size("seq"), lax.axis_index("seq")
    size = whole.shape[axis] // ways
    return tuple(pick(whole, (side + hop) % ways, size, axis) for hop in range(ways))


def swap_pieces(pieces):
    ways = lax.axis_size("seq")
    return pieces[:1] + tuple(
        lax.ppermute(piece, "seq", [(i, (i + hop) % ways) for i in range(ways)])
        for hop, piece in enumerate(pieces)
        if hop
    )


def start_items(array, per):
    return swap_pieces(split_items(array, per))


def joined_pieces(pieces, axis):
    ways, side = lax.axis_size("seq"), lax.axis_index("seq")
    if ways == 2:
        return ordered(pieces[0], pieces[1], side, axis)
    size = pieces[0].shape[axis]
    shape = list(pieces[0].shape)
    shape[axis] = size * ways
    whole = jnp.zeros(shape, pieces[0].dtype)
    for hop, piece in enumerate(pieces):
        source = (side - hop) % ways
        whole = lax.dynamic_update_slice_in_dim(whole, piece, source * size, axis)
    return whole


HINT = pl.CostEstimate(flops=10**13, transcendentals=0, bytes_accessed=10**9)


def block_loader(parts, offset, blocks, base, count, side, sems):
    size = blocks.shape[1]
    rows, columns = parts[0].shape
    first = pl.program_id(0) == 0
    copies = []
    for b in range(count):
        copies.append([])
        target = base + b
        if len(parts) == 1:
            row, column = divmod(b, columns // size)
            source = parts[0].at[pl.ds(row * size, size), pl.ds(column * size, size)]
            copy = pltpu.make_async_copy(source, blocks.at[target], sems.at[0, target])
            copies[b].append((first, copy))
        elif rows >= size:
            half, place = divmod(b, rows // size)
            for p, part in enumerate(parts):
                mine = side == half if p == 0 else side != half
                source = part.at[pl.ds(place * size, size), :]
                copy = pltpu.make_async_copy(
                    source, blocks.at[target], sems.at[0, target]
                )
                copies[b].append((jnp.logical_and(first, mine), copy))
        else:
            for p, part in enumerate(parts):
                start = pl.multiple_of((side if p == 0 else 1 - side) * rows, 16)
                column = (b + (offset if p else 0)) * size
                copy = pltpu.make_async_copy(
                    part.at[:, pl.ds(column, size)],
                    blocks.at[target, pl.ds(start, rows), :],
                    sems.at[p, target],
                )
                copies[b].append((first, copy))
    for pair in copies:
        for when, copy in pair:
            pl.when(when)(copy.start)
    return copies


def dense(name, body, rows_in, vectors, weights, outs, sums=(), steps=2):
    rows = rows_in[0].shape[0]
    tile = rows // steps
    total = sum(count for count, _, _ in weights)
    arrays = [part for _, _, parts in weights for part in parts]
    cuts = [len(rows_in), len(vectors), len(arrays), len(outs), len(sums)]

    def kernel(side, *refs):
        groups = []
        for size in cuts:
            groups.append(refs[:size])
            refs = refs[size:]
        blocks, sems = refs
        copies, parts = [], groups[2]
        for count, offset, used in weights:
            copies += block_loader(
                parts[: len(used)], offset, blocks, len(copies), count, side[0], sems
            )
            parts = parts[len(used) :]

        def wait(b):
            for when, copy in copies[b]:
                pl.when(when)(copy.wait)

        if sums:

            @pl.when(pl.program_id(0) == 0)
            def _():
                for ref in groups[4]:
                    ref[...] = jnp.zeros_like(ref)

        body(wait, blocks, groups[0], groups[1], groups[3], groups[4])

    return pl.pallas_call(
        kernel,
        out_shape=tuple(jax.ShapeDtypeStruct((rows, c), d) for c, d in outs)
        + tuple(jax.ShapeDtypeStruct((1, c), F32) for c in sums),
        grid_spec=pltpu.PrefetchScalarGridSpec(
            num_scalar_prefetch=1,
            grid=(steps,),
            in_specs=[
                pl.BlockSpec((tile, a.shape[1]), lambda i, _: (i, 0)) for a in rows_in
            ]
            + [pl.BlockSpec(a.shape, lambda i, _: (0, 0)) for a in vectors]
            + [pl.BlockSpec(memory_space=pl.ANY) for _ in arrays],
            out_specs=tuple(pl.BlockSpec((tile, c), lambda i, _: (i, 0)) for c, _ in outs)
            + tuple(pl.BlockSpec((1, c), lambda i, _: (0, 0)) for c in sums),
            scratch_shapes=[
                pltpu.VMEM((total, WIDTH, WIDTH), BF16),
                pltpu.SemaphoreType.DMA((2, total)),
            ],
        ),
        compiler_params=pltpu.CompilerParams(vmem_limit_bytes=60 << 20),
        cost_estimate=HINT,
        name=name,
    )(lax.axis_index("seq").reshape(1), *rows_in, *vectors, *arrays)


def fold_kernel(index_ref, *refs):
    (*parts, sent, keep) = refs
    index = index_ref[0]

    def total(place):
        values = [part[0, place].astype(F32) for part in parts]
        return sum(values[1:], values[0]).astype(BF16)

    sent[0] = total(1 - index)
    keep[0] = total(index)


def fold(name, outer, lane, lanes, *parts):
    index = lax.axis_index(name).reshape(1)
    count, unit, columns = parts[0].shape
    inner = count // (2 * outer)
    size = columns // lanes
    half = jax.ShapeDtypeStruct((outer, inner, unit, size), BF16)
    out = pl.pallas_call(
        fold_kernel,
        out_shape=(half, half),
        grid_spec=pltpu.PrefetchScalarGridSpec(
            num_scalar_prefetch=1,
            grid=(outer, inner),
            in_specs=[
                pl.BlockSpec((1, 2, 1, unit, size), lambda i, j, _: (i, 0, j, 0, lane))
                for _ in parts
            ],
            out_specs=(
                pl.BlockSpec((1, 1, unit, size), lambda i, j, _: (i, j, 0, 0)),
            )
            * 2,
        ),
        compiler_params=pltpu.CompilerParams(vmem_limit_bytes=60 << 20),
        cost_estimate=HINT,
        name="fold_" + name,
    )(index, *(part.reshape(outer, 2, inner, unit, columns) for part in parts))
    return tuple(part.reshape(count // 2, unit, size) for part in out)


def add_kernel(*refs):
    (*parts, out) = refs
    size = parts[0].shape[1]
    for k in range(len(parts) // 2):
        total = parts[2 * k][...].astype(F32) + parts[2 * k + 1][...].astype(F32)
        out[:, k * size : (k + 1) * size] = total.astype(out.dtype)


def add(*parts):
    rows, columns = parts[0].shape
    return pl.pallas_call(
        add_kernel,
        out_shape=jax.ShapeDtypeStruct((rows, columns * len(parts) // 2), parts[0].dtype),
        compiler_params=pltpu.CompilerParams(vmem_limit_bytes=60 << 20),
        cost_estimate=HINT,
        name="add",
    )(*parts)


def widen_kernel(value, *outs):
    start = 0
    for out in outs:
        out[...] = value[:, start : start + out.shape[1]].astype(F32)
        start += out.shape[1]


def widen(cuts, value):
    rows, columns = value.shape
    steps = 4 if rows % 32 == 0 else 2
    return pl.pallas_call(
        widen_kernel,
        out_shape=tuple(jax.ShapeDtypeStruct((rows, size), F32) for size in cuts),
        grid=(steps,),
        in_specs=[pl.BlockSpec((rows // steps, columns), lambda i: (i, 0))],
        out_specs=tuple(
            pl.BlockSpec((rows // steps, size), lambda i: (i, 0)) for size in cuts
        ),
        compiler_params=pltpu.CompilerParams(vmem_limit_bytes=60 << 20),
        cost_estimate=HINT,
        name="widen",
    )(value)


def eighth_copy_kernel(place, shard, out):
    out[...] = shard[...]


def eighth_copy(shard):
    rows, columns = shard.shape[0] // 8, shard.shape[1]
    place = lax.axis_index("z") * 4 + lax.axis_index("x") * 2 + lax.axis_index("c")
    return pl.pallas_call(
        eighth_copy_kernel,
        out_shape=jax.ShapeDtypeStruct((rows, columns), BF16),
        grid_spec=pltpu.PrefetchScalarGridSpec(
            num_scalar_prefetch=1,
            grid=(1,),
            in_specs=[pl.BlockSpec((rows, columns), lambda i, place: (place[0], 0))],
            out_specs=pl.BlockSpec((rows, columns), lambda i, place: (0, 0)),
        ),
        compiler_params=pltpu.CompilerParams(vmem_limit_bytes=60 << 20),
        cost_estimate=HINT,
        name="eighth",
    )(place.reshape(1), shard)


def normalize(hidden):
    mean_val = jnp.mean(hidden, -1, keepdims=True)
    centred = hidden - mean_val
    scale = lax.rsqrt(jnp.mean(centred * centred, -1, keepdims=True) + EPS)
    return centred * scale, scale


def add_sum(ref, values):
    ref[...] += jnp.sum(values, 0, keepdims=True)


def columns_of(b):
    return slice(b * WIDTH, (b + 1) * WIDTH)


def base_inward_body(wait, blocks, rows, vectors, outs, sums):
    wait(0)
    total = simple(rows[0][...], blocks[0])
    wait(1)
    total = total + simple(rows[1][...], blocks[1]) + vectors[0][...]
    outs[0][...] = total
    normed = (normalize(total)[0] * vectors[1][...] + vectors[2][...]).astype(BF16)
    outs[1][...] = normed
    for b in range(3):
        wait(2 + b)
        outs[2][:, columns_of(b)] = simple(outs[1][...], blocks[2 + b]).astype(BF16)


def middle_expand_body(wait, blocks, rows, vectors, outs, sums):
    wait(0)
    total = simple(rows[0][...], blocks[0]) + rows[1][...] + vectors[0][...]
    outs[0][...] = total
    normed = (normalize(total)[0] * vectors[1][...] + vectors[2][...]).astype(BF16)
    outs[1][...] = normed
    for b in range(4):
        wait(1 + b)
        upper = simple(outs[1][...], blocks[1 + b]) + vectors[3][:, columns_of(b)]
        below = 0.5 * (1.0 + lax.erf(upper * 0.7071067811865476))
        bell = jnp.exp(-0.5 * upper * upper) * 0.3989422804014327
        outs[2][:, columns_of(b)] = (upper * below).astype(BF16)
        outs[3][:, columns_of(b)] = (below + upper * bell).astype(BF16)


def contract_body(wait, blocks, rows, vectors, outs, sums):
    total = rows[1][...] + vectors[0][...]
    for b in range(blocks.shape[0]):
        wait(b)
        total = total + simple(rows[0][:, columns_of(b)], blocks[b])
    outs[0][...] = total.astype(BF16)


def upper_back_body(wait, blocks, rows, vectors, outs, sums):
    grad = rows[0][...]
    add_sum(sums[1], grad.astype(F32))
    for b in range(blocks.shape[0]):
        wait(b)
        upper = against(grad, blocks[b]) * rows[1][:, columns_of(b)].astype(F32)
        upper = upper.astype(BF16)
        outs[0][:, columns_of(b)] = upper
        add_sum(sums[0].at[:, columns_of(b)], upper.astype(F32))


def norm_back_body(count, wait, blocks, rows, vectors, outs, sums):
    grad = None
    for b in range(count):
        wait(b)
        part = against(rows[0][:, columns_of(b)], blocks[b])
        grad = part if grad is None else grad + part
    xhat, scale = normalize(rows[1][...])
    inner = grad * vectors[0][...]
    back = scale * (
        inner
        - jnp.mean(inner, -1, keepdims=True)
        - xhat * jnp.mean(inner * xhat, -1, keepdims=True)
    )
    total = rows[2][...].astype(F32) + back
    rounded = total.astype(BF16)
    outs[0][...] = rounded
    add_sum(sums[0], grad * xhat)
    add_sum(sums[1], grad)
    add_sum(sums[2], rounded.astype(F32))
    if len(outs) > 1:
        outs[1][...] = total
        wait(count)
        outs[2][...] = against(outs[0][...], blocks[count]).astype(BF16)


def against_body(wait, blocks, rows, vectors, outs, sums):
    for b in range(blocks.shape[0]):
        wait(b)
        result = against(rows[0][...], blocks[b]).astype(BF16)
        size = outs[b].shape[1]
        outs[b][...] = result[:, :size]
        if size < WIDTH:
            outs[b + 1][...] = result[:, size:]


def core_gradients(name, core, lefts, rights):
    rows = rights[0].shape[0]
    columns = sum(right.shape[1] for right in rights)
    stacked = len(rights) == 1
    depth = sum(left.shape[1] for left in lefts) if stacked else WIDTH
    tiles, unit = depth // WIDTH, depth // 16
    per = WIDTH // unit // 2
    count = len(lefts)
    ends = [0]
    for array in lefts if stacked else rights:
        ends.append(ends[-1] + array.shape[1] // WIDTH)

    def kernel(core_ref, *refs):
        left, right = refs[:count], refs[count : count + len(rights)]
        sent, keep = refs[count + len(rights) :]

        def run(left_ref, right_ref):
            grad = across(left_ref[...], right_ref[...])
            second = core_ref[0] == 1
            for j in range(0, 2 * per, 2):
                even = grad[j * unit : (j + 1) * unit].astype(BF16)
                odd = grad[(j + 1) * unit : (j + 2) * unit].astype(BF16)
                keep[j // 2] = jnp.where(second, odd, even)
                sent[j // 2] = jnp.where(second, even, odd)

        if count == 1:
            run(left[0], right[0])
        else:
            place = pl.program_id(0 if stacked else 1)
            for k in range(count):
                here = jnp.logical_and(place >= ends[k], place < ends[k + 1])
                pl.when(here)(
                    functools.partial(run, left[k], right[0 if stacked else k])
                )

    def clipped(index, k, blocks):
        return jnp.clip(index - ends[k], 0, blocks - 1)

    def left_spec(k, left):
        blocks = left.shape[1] // WIDTH
        if stacked:
            return pl.BlockSpec(
                (rows, WIDTH), lambda i, n, _: (0, clipped(i, k, blocks))
            )
        return pl.BlockSpec((rows, WIDTH), lambda i, n, _: (0, 0))

    def right_spec(k, right):
        blocks = right.shape[1] // WIDTH
        if stacked:
            return pl.BlockSpec((rows, WIDTH), lambda i, n, _: (0, n))
        return pl.BlockSpec((rows, WIDTH), lambda i, n, _: (0, clipped(n, k, blocks)))

    half = jax.ShapeDtypeStruct((8, unit, columns), BF16)
    return pl.pallas_call(
        kernel,
        out_shape=(half, half),
        grid_spec=pltpu.PrefetchScalarGridSpec(
            num_scalar_prefetch=1,
            grid=(tiles, columns // WIDTH),
            in_specs=[left_spec(k, left) for k, left in enumerate(lefts)]
            + [right_spec(k, right) for k, right in enumerate(rights)],
            out_specs=(pl.BlockSpec((per, unit, WIDTH), lambda i, n, _: (i, 0, n)),) * 2,
        ),
        compiler_params=pltpu.CompilerParams(vmem_limit_bytes=60 << 20),
        cost_estimate=HINT,
        name=name,
    )(core, *lefts, *rights)


def head_window(head):
    start = head * HEAD_DIM
    first = start // LANES * LANES
    size = LANES if start + HEAD_DIM <= first + LANES else 2 * LANES
    return first, size, start - first


def head_mask(size, offset):
    lane = lax.broadcasted_iota(jnp.int32, (1, size), 1)
    return (lane >= offset) & (lane < offset + HEAD_DIM)


def head_groups(width, slots):
    heads = [(head,) + head_window(head) for head in range(width // HEAD_DIM)]
    count = max(1, 2048 // slots)
    return [heads[i : i + count] for i in range(0, len(heads), count)]


def masked(ref, first, size, offset):
    return jnp.where(head_mask(size, offset), ref[:, first : first + size], 0)


def place(ref, start, size, offset, result):
    result = result.astype(BF16)
    if offset:
        result = jnp.where(
            head_mask(size, offset), result, ref[:, start : start + size]
        )
    ref[:, start : start + size] = result


def attend_kernel(lengths, qkv, mixed, probs_out):
    slots, width = mixed.shape
    live = lax.broadcasted_iota(jnp.int32, (1, slots), 1) < lengths[pl.program_id(0)]
    for group in head_groups(width, slots):
        scores = [
            against(
                masked(qkv, first, size, offset),
                qkv[:, width + first : width + first + size],
            )
            for _, first, size, offset in group
        ]
        scores = [jnp.where(live, s * HEAD_DIM ** (-0.5), NEG) for s in scores]
        raised = [jnp.exp(s - jnp.max(s, -1, keepdims=True)) for s in scores]
        probs = [
            (r * (1.0 / jnp.sum(r, -1, keepdims=True))).astype(BF16) for r in raised
        ]
        results = [
            simple(p, qkv[:, 2 * width + first : 2 * width + first + size])
            for p, (_, first, size, _) in zip(probs, group)
        ]
        for p, result, (head, first, size, offset) in zip(probs, results, group):
            probs_out[head * slots : (head + 1) * slots, :] = p
            place(mixed, first, size, offset, result)


def attend(qkv, lengths):
    per = lengths.shape[0]
    rows, width = qkv.shape[0], qkv.shape[1] // 3
    slots, heads = rows // per, width // HEAD_DIM
    return pl.pallas_call(
        attend_kernel,
        out_shape=(
            jax.ShapeDtypeStruct((rows, width), BF16),
            jax.ShapeDtypeStruct((rows * heads, slots), BF16),
        ),
        grid_spec=pltpu.PrefetchScalarGridSpec(
            num_scalar_prefetch=1,
            grid=(per,),
            in_specs=[pl.BlockSpec((slots, 3 * width), lambda i, _: (i, 0))],
            out_specs=(
                pl.BlockSpec((slots, width), lambda i, _: (i, 0)),
                pl.BlockSpec((heads * slots, slots), lambda i, _: (i, 0)),
            ),
        ),
        compiler_params=pltpu.CompilerParams(vmem_limit_bytes=60 << 20),
        cost_estimate=HINT,
        name="attend",
    )(lengths, qkv)


def attend_back_kernel(qkv, probs_in, grad_mixed, grad_qkv):
    slots, width = grad_mixed.shape
    scale = HEAD_DIM ** (-0.5)
    for group in head_groups(width, slots):
        grads = [masked(grad_mixed, *window) for _, *window in group]
        grad_probs = [
            against(g, qkv[:, 2 * width + first : 2 * width + first + size])
            for g, (_, first, size, _) in zip(grads, group)
        ]
        probs = [
            probs_in[head * slots : (head + 1) * slots, :] for head, _, _, _ in group
        ]
        grad_values = [across(p, g) for p, g in zip(probs, grads)]
        probs = [p.astype(F32) for p in probs]
        sums = [
            jnp.sum(g * p, -1, keepdims=True) for g, p in zip(grad_probs, probs)
        ]
        scores = [
            (p * (g - total)).astype(BF16)
            for p, g, total in zip(probs, grad_probs, sums)
        ]
        grad_queries = [
            simple(s, qkv[:, width + first : width + first + size]) * scale
            for s, (_, first, size, _) in zip(scores, group)
        ]
        grad_keys = [
            across(s, qkv[:, first : first + size]) * scale
            for s, (_, first, size, _) in zip(scores, group)
        ]
        for part, results in enumerate((grad_queries, grad_keys, grad_values)):
            for result, (_, first, size, offset) in zip(results, group):
                place(grad_qkv, part * width + first, size, offset, result)


def attend_back(qkv, probs, grad_mixed, per):
    rows, width = grad_mixed.shape
    slots, heads = rows // per, width // HEAD_DIM
    return pl.pallas_call(
        attend_back_kernel,
        out_shape=jax.ShapeDtypeStruct((rows, 3 * width), BF16),
        grid=(per,),
        in_specs=[
            pl.BlockSpec((slots, 3 * width), lambda i: (i, 0)),
            pl.BlockSpec((heads * slots, slots), lambda i: (i, 0)),
            pl.BlockSpec((slots, width), lambda i: (i, 0)),
        ],
        out_specs=pl.BlockSpec((slots, 3 * width), lambda i: (i, 0)),
        compiler_params=pltpu.CompilerParams(vmem_limit_bytes=60 << 20),
        cost_estimate=HINT,
        name="attend_back",
    )(qkv, probs, grad_mixed)


def per_device(
    latents,
    skip_store,
    lengths,
    cotangent,
    skip_weight,
    skip_bias,
    first_gain,
    first_shift,
    inward_weight,
    outward_weight,
    outward_bias,
    second_gain,
    second_shift,
    expand_weight,
    expand_bias,
    contract_weight,
    contract_bias,
):
    items, slot_dev, width = latents.shape
    ways, side = lax.axis_size("seq"), lax.axis_index("seq")
    slots = slot_dev * ways
    per = -(-items // ways)
    rows = per * slots
    fast = fast_mesh()
    chain = Chain()

    live = jnp.pad(lengths, (0, per * ways - items), constant_values=slots)
    live = pick(live, side, per)

    small = (
        skip_bias,
        first_gain,
        first_shift,
        outward_bias,
        second_gain,
        second_shift,
        expand_bias,
        contract_bias,
    )
    if fast:
        skip_piece = flip(chain.run(eighth, skip_weight), "seq")
        attention_piece = flip(
            chain.run(
                lambda a, b: jnp.concatenate([eighth(a), eighth(b)], 1),
                inward_weight,
                outward_weight,
            ),
            "seq",
        )
        vectors = gather_vectors(chain, small)
        expand_piece = flip(chain.run(eighth, expand_weight), "seq")
        skip_pieces = chain.run(lambda a: start_items(a, per), skip_store)
        latent_pieces = chain.run(lambda a: start_items(a, per), latents)
        skip_parts = (skip_weight, share(*chain.enter(skip_piece)))
        attention_other = share(*chain.enter(attention_piece))
        inward_parts = (inward_weight, attention_other)
        outward_parts = (outward_weight, attention_other)
        grad_pieces = chain.run(lambda a: split_items(a, per), cotangent)
        skip_rows = chain.run(
            lambda *a: joined_pieces(a, 2).reshape(rows, width), *skip_pieces
        )
        expand_parts = (expand_weight, share(*chain.enter(expand_piece)))
        contract_piece = chain.run(eighth_copy, contract_weight)
        latent_rows = chain.run(
            lambda *a: joined_pieces(a, 1).reshape(rows, width), *latent_pieces
        )
        contract_piece = flip(*chain.enter(contract_piece), "seq")
        grad_pieces = swap_pieces(chain.enter(*grad_pieces))
    else:
        skip_parts, inward_parts, outward_parts, expand_parts, contract_parts = (
            (lax.all_gather(shard, "seq", axis=0, tiled=True),)
            for shard in (
                skip_weight,
                inward_weight,
                outward_weight,
                expand_weight,
                contract_weight,
            )
        )
        skip_rows = joined_pieces(start_items(skip_store, per), 2)
        latent_rows = joined_pieces(start_items(latents, per), 1)
        grad_pieces = start_items(cotangent, per)
        vectors = gather_vectors(chain, small)
    (
        skip_offset,
        gain_first,
        shift_first,
        outward_offset,
        gain_second,
        shift_second,
        expand_offset,
        contract_offset,
    ) = vectors
    skip_matrix, inward_matrix = (2, 0, skip_parts), (3, 0, inward_parts)
    outward_matrix = (1, 3, outward_parts)
    skip_rows, latent_rows = (a.reshape(rows, width) for a in (skip_rows, latent_rows))
    one, wide = (width, BF16), (width, F32)
    hidden = (expand_offset.shape[1], BF16)

    base, first_normed, qkv_vals = chain.run(
        lambda *a: dense(
            "base_inward",
            base_inward_body,
            a,
            (skip_offset, gain_first, shift_first),
            (skip_matrix, inward_matrix),
            [wide, one, (3 * width, BF16)],
        ),
        latent_rows,
        skip_rows,
    )
    mixed_rows, probs = chain.run(lambda a: attend(a, live), qkv_vals)
    if fast:
        contract_parts = (contract_weight, share(*chain.enter(contract_piece)))
    expand_matrix, contract_matrix = (4, 0, expand_parts), (4, 0, contract_parts)
    grad_out = chain.run(
        lambda *a: joined_pieces(a, 1).reshape(rows, width), *grad_pieces
    )
    middle, second_normed, activated, slope = chain.run(
        lambda *a: dense(
            "middle_expand",
            middle_expand_body,
            a,
            (outward_offset, gain_second, shift_second, expand_offset),
            (outward_matrix, expand_matrix),
            [wide, one, hidden, hidden],
            steps=4,
        ),
        mixed_rows,
        base,
    )
    contract_sum = Reduction(chain, "contract_grad", (activated,), (grad_out,))
    grad_upper, grad_expand_off, grad_contract_off = chain.run(
        lambda *a: dense(
            "upper_back",
            upper_back_body,
            a,
            (),
            (contract_matrix,),
            [hidden],
            [hidden[0], width],
        ),
        grad_out,
        slope,
    )
    contract_sum.step()
    expand_sum = Reduction(chain, "expand_grad", (second_normed,), (grad_upper,))
    (
        grad_branch,
        grad_middle,
        grad_mixed,
        grad_gain_two,
        grad_shift_two,
        grad_outward_off,
    ) = chain.run(
        lambda *a: dense(
            "middle_back",
            functools.partial(norm_back_body, 4),
            a,
            (gain_second,),
            (expand_matrix, outward_matrix),
            [one, wide, one],
            [width] * 3,
        ),
        grad_upper,
        middle,
        grad_out,
    )
    expand_sum.step()
    contract_sum.step()
    grad_qkv = chain.run(lambda a: attend_back(qkv_vals, probs, a, per), grad_mixed)
    attention_sum = Reduction(
        chain,
        "attention_grad",
        (first_normed, mixed_rows),
        (grad_qkv, grad_branch),
        lanes=2,
    )
    contract_sum.step()
    grad_base, grad_gain_one, grad_shift_one, grad_skip_off = chain.run(
        lambda *a: dense(
            "base_back",
            functools.partial(norm_back_body, 3),
            a,
            (gain_first,),
            (inward_matrix,),
            [one],
            [width] * 3,
        ),
        grad_qkv,
        base,
        grad_middle,
    )
    expand_sum.step()
    contract_sum.step()
    attention_sum.step(1)
    attention_sum.step(0)
    skip_sum = Reduction(chain, "skip_grad", (latent_rows, skip_rows), (grad_base,))
    expand_sum.step()
    skip_sum.step()
    contract_sum.step()
    attention_sum.step(0)
    expand_sum.step()
    vector_sum = VectorReduction(
        chain,
        (
            grad_skip_off,
            grad_gain_one,
            grad_shift_one,
            grad_outward_off,
            grad_gain_two,
            grad_shift_two,
            grad_expand_off,
            grad_contract_off,
        ),
    )
    attention_sum.step(0)
    vector_sum.step()
    attention_sum.step(1)
    attention_sum.step(0)
    expand_sum.step()
    attention_sum.step(1)
    vector_sum.step()
    halves = ways == 2
    columns = [width] + ([width // 2] * 2 if halves else [width])
    grad_latents, *grad_skip = chain.run(
        lambda a: dense(
            "joined_back",
            against_body,
            (a,),
            (),
            (skip_matrix,),
            [(size, BF16) for size in columns],
        ),
        grad_base,
    )
    latent_pieces = chain.run(
        lambda a: split_parts(a.reshape(per, slots, width), 1), grad_latents
    )
    if halves:
        skip_pieces = chain.run(
            lambda a, b: (jnp.where(side == 0, a, b), jnp.where(side == 0, b, a)),
            *grad_skip,
        )
        skip_pieces = tuple(a.reshape(per, slots, width // 2) for a in skip_pieces)
    else:
        skip_pieces = split_parts(grad_skip[0].reshape(per, slots, width), 2)
    attention_sum.step(1)
    skip_sum.step()
    vector_sum.step()
    latent_pieces = swap_pieces(chain.enter(*latent_pieces))
    skip_pieces = swap_pieces(chain.enter(*skip_pieces))
    (sum_contract,) = contract_sum.finish()
    skip_sum.step()
    vector_sum.step()
    attention_sum.join()
    skip_sum.step()
    (result,) = chain.run(
        lambda *a: dense(
            "contract",
            contract_body,
            a,
            (contract_offset,),
            (contract_matrix,),
            [one],
            steps=4,
        ),
        activated,
        middle,
    )
    grad_latents = chain.run(
        lambda *a: joined_pieces(a, 0)[:items].astype(F32), *latent_pieces
    )
    skip_sum.step()
    grad_skip = chain.run(lambda *a: joined_pieces(a, 0)[:items], *skip_pieces)
    output_pieces = chain.run(
        lambda a: split_parts(a.reshape(per, slots, width), 1), result
    )
    output_pieces = swap_pieces(output_pieces)
    (sum_expand,) = expand_sum.finish()
    vector_sum.step()
    sum_inward, sum_outward = attention_sum.finish()
    (sum_skipw,) = skip_sum.finish()
    output = chain.run(lambda *a: joined_pieces(a, 0)[:items], *output_pieces)
    (
        sum_skipb,
        sum_gain1,
        sum_shift1,
        sum_outb,
        sum_gain2,
        sum_shift2,
        sum_expandb,
        sum_contractb,
    ) = vector_sum.finish()
    return (
        output,
        grad_latents,
        grad_skip,
        sum_skipw,
        sum_skipb,
        sum_gain1,
        sum_shift1,
        sum_inward,
        sum_outward,
        sum_outb,
        sum_gain2,
        sum_shift2,
        sum_expand,
        sum_expandb,
        sum_contract,
        sum_contractb,
    )


def solution(mesh):
    wide, seq = mesh.shape["wide"], mesh.shape["seq"]
    devices = mesh.devices.reshape(wide // 8, 2, 2, 2, seq)
    return jax.shard_map(
        per_device,
        mesh=Mesh(devices, WIDE + ("seq",)),
        in_specs=(
            P(WIDE, "seq", None),
            P(WIDE, None, "seq"),
            P(WIDE),
            P(WIDE, "seq", None),
            P("seq", None),
            P("seq"),
            P("seq"),
            P("seq"),
            P("seq", None),
            P("seq", None),
            P("seq"),
            P("seq"),
            P("seq"),
            P("seq", None),
            P("seq"),
            P("seq", None),
            P("seq"),
        ),
        out_specs=(
            P(WIDE, "seq", None),
            P(WIDE, "seq", None),
            P(WIDE, None, "seq"),
            P("seq", None),
            P("seq"),
            P("seq"),
            P("seq"),
            P("seq", None),
            P("seq", None),
            P("seq"),
            P("seq"),
            P("seq"),
            P("seq", None),
            P("seq"),
            P("seq", None),
            P("seq"),
        ),
        check_vma=False,
    )
```

```python
import functools

import jax
import jax.numpy as jnp
from jax import lax
from jax.experimental import pallas as pl
from jax.experimental.pallas import tpu as pltpu
from jax.sharding import Mesh
from jax.sharding import PartitionSpec as P

HEAD_DIM = 72
WIDTH = 16 * HEAD_DIM

EPS = 1e-05
NEG = -1e30
PLANE = ("z", "x", "c")
WIDE = ("w",) + PLANE
BF16 = jnp.bfloat16
F32 = jnp.float32
LANES = 128

def across(left_side, right_side):
    return lax.dot_general(
        left_side, right_side, (((0,), (0,)), ((), ())), preferred_element_type=F32
    )


def against(left_side, right_side):
    return lax.dot_general(
        left_side, right_side, (((1,), (1,)), ((), ())), preferred_element_type=F32
    )


def simple(left_side, right_side):
    return jnp.dot(left_side, right_side, preferred_element_type=F32)


def pick(array, index, size, axis=0):
    return lax.dynamic_slice_in_dim(array, index * size, size, axis)


def flip(array, axis):
    return lax.ppermute(array, axis, [(0, 1), (1, 0)])


def ordered(mine, other, index, axis=0):
    return jnp.where(
        index == 0,
        jnp.concatenate([mine, other], axis),
        jnp.concatenate([other, mine], axis),
    )


class Chain:
    def __init__(self):
        self.last = ()

    def enter(self, *values):
        values = lax.optimization_barrier(values + self.last)[: len(values)]
        return values

    def leave(self, *values):
        self.last = values[:1]
        return values if len(values) > 1 else values[0]

    def run(self, function, *values):
        out = function(*self.enter(*values))
        self.last = tuple(out)[:1] if isinstance(out, (tuple, list)) else (out,)
        return out


def fast_mesh():
    return lax.axis_size("seq") == 2 and lax.axis_size("w") == 2


def block(array, index, axis):
    return lax.dynamic_index_in_dim(array, index, axis, keepdims=False)


def eighth(shard):
    place = lax.axis_index("z") * 4 + lax.axis_index("x") * 2 + lax.axis_index("c")
    return pick(shard, place, shard.shape[0] // 8)


def share(piece):
    return lax.all_gather(piece, PLANE, axis=0, tiled=True)


class Reduction:
    def __init__(self, chain, name, lefts, rights, lanes=1):
        self.chain, self.lanes = chain, lanes
        self.cuts = [right.shape[1] for right in rights]
        if fast_mesh():
            core = lax.axis_index("c").reshape(1)
            count = len(lefts)
            sent, keep = chain.run(
                lambda *a: core_gradients(name, core, a[:count], a[count:]),
                *lefts,
                *rights,
            )
            self.parts = [(keep, flip(sent, "c"))] * lanes
            self.names = [["seq", "x", "z", "w"] for _ in range(lanes)]
        else:
            axis = int(len(rights) > 1)
            pairs = zip(lefts, rights) if axis else ((a, rights[0]) for a in lefts)
            grad = jnp.concatenate([across(*p).astype(BF16) for p in pairs], axis)
            part = lax.psum_scatter(grad, "seq", scatter_dimension=0, tiled=True)
            self.total, self.names = lax.psum(part, WIDE), None

    def step(self, lane=0):
        if self.names is None:
            return
        if not self.names[lane]:
            self.join()
            return
        name, parts = self.names[lane].pop(0), self.parts[lane]
        if name == "w":
            sent = self.chain.run(
                lambda *a: add(*(part.reshape(part.shape[1:]) for part in a)), *parts
            )
            self.parts[lane] = (sent, flip(sent, name))
        else:
            outer = 2 if name == "x" else 1
            lanes = self.lanes if name == "seq" else 1
            sent, keep = self.chain.run(
                functools.partial(fold, name, outer, lane if lanes > 1 else 0, lanes),
                *parts,
            )
            self.parts[lane] = (keep, flip(sent, name))

    def join(self):
        if self.names is None:
            return
        assert not any(self.names)
        parts = [part for pair in self.parts for part in pair]
        self.total = share(self.chain.run(add, *parts))

    def finish(self):
        return self.chain.run(functools.partial(widen, self.cuts), self.total)


def gather_vectors(chain, vectors):
    joined = chain.run(lambda *a: jnp.concatenate(a), *vectors)
    mine = joined.reshape(1, -1)
    if fast_mesh():
        everything = ordered(mine, flip(mine, "seq"), lax.axis_index("seq"))
    else:
        everything = lax.all_gather(mine, "seq", axis=0, tiled=True)
    out, start = [], 0
    for vector in vectors:
        size = vector.shape[0]
        out.append(everything[:, start : start + size].reshape(1, -1).astype(F32))
        start += size
    return out


class VectorReduction:
    def __init__(self, chain, vectors):
        self.chain, self.sizes = chain, [vector.shape[1] for vector in vectors]
        self.total = chain.run(lambda *a: jnp.concatenate(a, 1), *vectors)
        self.names = ["c", "x", "z", "w", "seq"]
        if fast_mesh():
            self.got = flip(self.total, self.names.pop(0))
        else:
            self.total, self.names = lax.psum(self.total, WIDE + ("seq",)), []

    def step(self):
        if fast_mesh():
            self.total = self.chain.run(add, self.total, self.got)
            if self.names:
                self.got = flip(self.total, self.names.pop(0))

    def finish(self):
        assert not self.names
        ways, side = lax.axis_size("seq"), lax.axis_index("seq")
        out, start = [], 0
        for whole in self.sizes:
            size = whole // ways
            shards = self.total[:, start : start + whole].reshape(ways, size)
            out.append(block(shards, side, 0))
            start += whole
        return out


def split_items(array, per):
    ways, side = lax.axis_size("seq"), lax.axis_index("seq")
    padding = [(0, per * ways - array.shape[0])] + [(0, 0)] * (array.ndim - 1)
    array = jnp.pad(array, padding)
    return tuple(pick(array, (side + hop) % ways, per) for hop in range(ways))


def split_parts(whole, axis):
    ways, side = lax.axis_size("seq"), lax.axis_index("seq")
    size = whole.shape[axis] // ways
    return tuple(pick(whole, (side + hop) % ways, size, axis) for hop in range(ways))


def swap_pieces(pieces):
    ways = lax.axis_size("seq")
    return pieces[:1] + tuple(
        lax.ppermute(piece, "seq", [(i, (i + hop) % ways) for i in range(ways)])
        for hop, piece in enumerate(pieces)
        if hop
    )


def start_items(array, per):
    return swap_pieces(split_items(array, per))


def joined_pieces(pieces, axis):
    ways, side = lax.axis_size("seq"), lax.axis_index("seq")
    if ways == 2:
        return ordered(pieces[0], pieces[1], side, axis)
    size = pieces[0].shape[axis]
    shape = list(pieces[0].shape)
    shape[axis] = size * ways
    whole = jnp.zeros(shape, pieces[0].dtype)
    for hop, piece in enumerate(pieces):
        source = (side - hop) % ways
        whole = lax.dynamic_update_slice_in_dim(whole, piece, source * size, axis)
    return whole


HINT = pl.CostEstimate(flops=10**13, transcendentals=0, bytes_accessed=10**9)


def block_loader(parts, offset, blocks, base, count, side, sems):
    size = blocks.shape[1]
    rows, columns = parts[0].shape
    first = pl.program_id(0) == 0
    copies = []
    for b in range(count):
        copies.append([])
        target = base + b
        if len(parts) == 1:
            row, column = divmod(b + offset, columns // size)
            source = parts[0].at[pl.ds(row * size, size), pl.ds(column * size, size)]
            copy = pltpu.make_async_copy(source, blocks.at[target], sems.at[0, target])
            copies[b].append((first, copy))
        elif rows >= size:
            half, place = divmod(b + offset, rows // size)
            for p, part in enumerate(parts):
                mine = side == half if p == 0 else side != half
                source = part.at[pl.ds(place * size, size), :]
                copy = pltpu.make_async_copy(
                    source, blocks.at[target], sems.at[0, target]
                )
                copies[b].append((jnp.logical_and(first, mine), copy))
        else:
            for p, part in enumerate(parts):
                start = pl.multiple_of((side if p == 0 else 1 - side) * rows, 16)
                column = (b + (offset if p else 0)) * size
                copy = pltpu.make_async_copy(
                    part.at[:, pl.ds(column, size)],
                    blocks.at[target, pl.ds(start, rows), :],
                    sems.at[p, target],
                )
                copies[b].append((first, copy))
    for pair in copies:
        for when, copy in pair:
            pl.when(when)(copy.start)
    return copies


def dense(name, body, rows_in, vectors, weights, outs, sums=(), steps=2):
    rows = rows_in[0].shape[0]
    tile = rows // steps
    total = sum(count for count, _, _ in weights)
    arrays = [part for _, _, parts in weights for part in parts]
    cuts = [len(rows_in), len(vectors), len(arrays), len(outs), len(sums)]

    def kernel(side, *refs):
        groups = []
        for size in cuts:
            groups.append(refs[:size])
            refs = refs[size:]
        blocks, sems = refs
        copies, parts = [], groups[2]
        for count, offset, used in weights:
            copies += block_loader(
                parts[: len(used)], offset, blocks, len(copies), count, side[0], sems
            )
            parts = parts[len(used) :]

        def wait(b):
            for when, copy in copies[b]:
                pl.when(when)(copy.wait)

        if sums:

            @pl.when(pl.program_id(0) == 0)
            def _():
                for ref in groups[4]:
                    ref[...] = jnp.zeros_like(ref)

        body(wait, blocks, groups[0], groups[1], groups[3], groups[4])

    return pl.pallas_call(
        kernel,
        out_shape=tuple(jax.ShapeDtypeStruct((rows, c), d) for c, d in outs)
        + tuple(jax.ShapeDtypeStruct((1, c), F32) for c in sums),
        grid_spec=pltpu.PrefetchScalarGridSpec(
            num_scalar_prefetch=1,
            grid=(steps,),
            in_specs=[
                pl.BlockSpec((tile, a.shape[1]), lambda i, _: (i, 0)) for a in rows_in
            ]
            + [pl.BlockSpec(a.shape, lambda i, _: (0, 0)) for a in vectors]
            + [pl.BlockSpec(memory_space=pl.ANY) for _ in arrays],
            out_specs=tuple(pl.BlockSpec((tile, c), lambda i, _: (i, 0)) for c, _ in outs)
            + tuple(pl.BlockSpec((1, c), lambda i, _: (0, 0)) for c in sums),
            scratch_shapes=[
                pltpu.VMEM((total, WIDTH, WIDTH), BF16),
                pltpu.SemaphoreType.DMA((2, total)),
            ],
        ),
        compiler_params=pltpu.CompilerParams(vmem_limit_bytes=60 << 20),
        cost_estimate=HINT,
        name=name,
    )(lax.axis_index("seq").reshape(1), *rows_in, *vectors, *arrays)


def fold_kernel(index_ref, *refs):
    (*parts, sent, keep) = refs
    index = index_ref[0]

    def total(place):
        values = [part[0, place].astype(F32) for part in parts]
        return sum(values[1:], values[0]).astype(BF16)

    sent[0] = total(1 - index)
    keep[0] = total(index)


def fold(name, outer, lane, lanes, *parts):
    index = lax.axis_index(name).reshape(1)
    count, unit, columns = parts[0].shape
    inner = count // (2 * outer)
    size, together = columns // lanes, min(inner, 2)
    half = jax.ShapeDtypeStruct((outer, inner, unit, size), BF16)
    out = pl.pallas_call(
        fold_kernel,
        out_shape=(half, half),
        grid_spec=pltpu.PrefetchScalarGridSpec(
            num_scalar_prefetch=1,
            grid=(outer, inner // together),
            in_specs=[
                pl.BlockSpec(
                    (1, 2, together, unit, size), lambda i, j, _: (i, 0, j, 0, lane)
                )
                for _ in parts
            ],
            out_specs=(
                pl.BlockSpec((1, together, unit, size), lambda i, j, _: (i, j, 0, 0)),
            )
            * 2,
        ),
        compiler_params=pltpu.CompilerParams(vmem_limit_bytes=60 << 20),
        cost_estimate=HINT,
        name="fold_" + name,
    )(index, *(part.reshape(outer, 2, inner, unit, columns) for part in parts))
    return tuple(part.reshape(count // 2, unit, size) for part in out)


def add_kernel(*refs):
    (*parts, out) = refs
    size = parts[0].shape[1]
    for k in range(len(parts) // 2):
        total = parts[2 * k][...].astype(F32) + parts[2 * k + 1][...].astype(F32)
        out[:, k * size : (k + 1) * size] = total.astype(out.dtype)


def add(*parts):
    rows, columns = parts[0].shape
    return pl.pallas_call(
        add_kernel,
        out_shape=jax.ShapeDtypeStruct((rows, columns * len(parts) // 2), parts[0].dtype),
        compiler_params=pltpu.CompilerParams(vmem_limit_bytes=60 << 20),
        cost_estimate=HINT,
        name="add",
    )(*parts)


def widen_kernel(value, *outs):
    start = 0
    for out in outs:
        out[...] = value[:, start : start + out.shape[1]].astype(F32)
        start += out.shape[1]


def widen(cuts, value):
    rows, columns = value.shape
    steps = 2
    return pl.pallas_call(
        widen_kernel,
        out_shape=tuple(jax.ShapeDtypeStruct((rows, size), F32) for size in cuts),
        grid=(steps,),
        in_specs=[pl.BlockSpec((rows // steps, columns), lambda i: (i, 0))],
        out_specs=tuple(
            pl.BlockSpec((rows // steps, size), lambda i: (i, 0)) for size in cuts
        ),
        compiler_params=pltpu.CompilerParams(vmem_limit_bytes=60 << 20),
        cost_estimate=HINT,
        name="widen",
    )(value)


def eighth_copy_kernel(place, shard, out):
    out[...] = shard[...]


def eighth_copy(shard):
    rows, columns = shard.shape[0] // 8, shard.shape[1]
    place = lax.axis_index("z") * 4 + lax.axis_index("x") * 2 + lax.axis_index("c")
    return pl.pallas_call(
        eighth_copy_kernel,
        out_shape=jax.ShapeDtypeStruct((rows, columns), BF16),
        grid_spec=pltpu.PrefetchScalarGridSpec(
            num_scalar_prefetch=1,
            grid=(1,),
            in_specs=[pl.BlockSpec((rows, columns), lambda i, place: (place[0], 0))],
            out_specs=pl.BlockSpec((rows, columns), lambda i, place: (0, 0)),
        ),
        compiler_params=pltpu.CompilerParams(vmem_limit_bytes=60 << 20),
        cost_estimate=HINT,
        name="eighth",
    )(place.reshape(1), shard)


def normalize(hidden):
    mean_val = jnp.mean(hidden, -1, keepdims=True)
    centred = hidden - mean_val
    scale = lax.rsqrt(jnp.mean(centred * centred, -1, keepdims=True) + EPS)
    return centred * scale, scale


def add_sum(ref, values):
    ref[...] += jnp.sum(values, 0, keepdims=True)


def columns_of(b):
    return slice(b * WIDTH, (b + 1) * WIDTH)


def skip_base_body(wait, blocks, rows, vectors, outs, sums):
    wait(0)
    outs[0][...] = simple(rows[0][...], blocks[0])


def base_inward_body(wait, blocks, rows, vectors, outs, sums):
    wait(0)
    total = simple(rows[0][...], blocks[0]) + rows[1][...] + vectors[0][...]
    outs[0][...] = total
    normed = (normalize(total)[0] * vectors[1][...] + vectors[2][...]).astype(BF16)
    outs[1][...] = normed
    for b in range(3):
        wait(1 + b)
        outs[2][:, columns_of(b)] = simple(outs[1][...], blocks[1 + b]).astype(BF16)


def middle_expand_body(wait, blocks, rows, vectors, outs, sums):
    wait(0)
    total = simple(rows[0][...], blocks[0]) + rows[1][...] + vectors[0][...]
    outs[0][...] = total
    normed = (normalize(total)[0] * vectors[1][...] + vectors[2][...]).astype(BF16)
    outs[1][...] = normed
    for b in range(4):
        wait(1 + b)
        upper = simple(outs[1][...], blocks[1 + b]) + vectors[3][:, columns_of(b)]
        below = 0.5 * (1.0 + lax.erf(upper * 0.7071067811865476))
        bell = jnp.exp(-0.5 * upper * upper) * 0.3989422804014327
        outs[2][:, columns_of(b)] = (upper * below).astype(BF16)
        outs[3][:, columns_of(b)] = (below + upper * bell).astype(BF16)


def contract_body(wait, blocks, rows, vectors, outs, sums):
    total = rows[1][...] + vectors[0][...]
    for b in range(blocks.shape[0]):
        wait(b)
        total = total + simple(rows[0][:, columns_of(b)], blocks[b])
    outs[0][...] = total.astype(BF16)


def upper_back_body(wait, blocks, rows, vectors, outs, sums):
    grad = rows[0][...]
    add_sum(sums[1], grad.astype(F32))
    for b in range(blocks.shape[0]):
        wait(b)
        upper = against(grad, blocks[b]) * rows[1][:, columns_of(b)].astype(F32)
        upper = upper.astype(BF16)
        outs[0][:, columns_of(b)] = upper
        add_sum(sums[0].at[:, columns_of(b)], upper.astype(F32))


def norm_back_body(count, wait, blocks, rows, vectors, outs, sums):
    grad = None
    for b in range(count):
        wait(b)
        part = against(rows[0][:, columns_of(b)], blocks[b])
        grad = part if grad is None else grad + part
    xhat, scale = normalize(rows[1][...])
    inner = grad * vectors[0][...]
    back = scale * (
        inner
        - jnp.mean(inner, -1, keepdims=True)
        - xhat * jnp.mean(inner * xhat, -1, keepdims=True)
    )
    total = rows[2][...].astype(F32) + back
    rounded = total.astype(BF16)
    outs[0][...] = rounded
    add_sum(sums[0], grad * xhat)
    add_sum(sums[1], grad)
    add_sum(sums[2], rounded.astype(F32))
    if len(outs) > 1:
        outs[1][...] = total
        wait(count)
        outs[2][...] = against(outs[0][...], blocks[count]).astype(BF16)


def against_body(wait, blocks, rows, vectors, outs, sums):
    for b in range(blocks.shape[0]):
        wait(b)
        result = against(rows[0][...], blocks[b]).astype(BF16)
        size = outs[b].shape[1]
        outs[b][...] = result[:, :size]
        if size < WIDTH:
            outs[b + 1][...] = result[:, size:]


def core_gradients(name, core, lefts, rights):
    rows = rights[0].shape[0]
    columns = sum(right.shape[1] for right in rights)
    stacked = len(rights) == 1
    depth = sum(left.shape[1] for left in lefts) if stacked else WIDTH
    tiles, unit = depth // WIDTH, depth // 16
    per = WIDTH // unit // 2
    count = len(lefts)
    ends = [0]
    for array in lefts if stacked else rights:
        ends.append(ends[-1] + array.shape[1] // WIDTH)

    def kernel(core_ref, *refs):
        left, right = refs[:count], refs[count : count + len(rights)]
        sent, keep = refs[count + len(rights) :]

        def run(left_ref, right_ref):
            grad = across(left_ref[...], right_ref[...])
            second = core_ref[0] == 1
            for j in range(0, 2 * per, 2):
                even = grad[j * unit : (j + 1) * unit].astype(BF16)
                odd = grad[(j + 1) * unit : (j + 2) * unit].astype(BF16)
                keep[j // 2] = jnp.where(second, odd, even)
                sent[j // 2] = jnp.where(second, even, odd)

        if count == 1:
            run(left[0], right[0])
        else:
            place = pl.program_id(0 if stacked else 1)
            for k in range(count):
                here = jnp.logical_and(place >= ends[k], place < ends[k + 1])
                pl.when(here)(
                    functools.partial(run, left[k], right[0 if stacked else k])
                )

    def clipped(index, k, blocks):
        return jnp.clip(index - ends[k], 0, blocks - 1)

    def left_spec(k, left):
        blocks = left.shape[1] // WIDTH
        if stacked:
            return pl.BlockSpec(
                (rows, WIDTH), lambda i, n, _: (0, clipped(i, k, blocks))
            )
        return pl.BlockSpec((rows, WIDTH), lambda i, n, _: (0, 0))

    def right_spec(k, right):
        blocks = right.shape[1] // WIDTH
        if stacked:
            return pl.BlockSpec((rows, WIDTH), lambda i, n, _: (0, n))
        return pl.BlockSpec((rows, WIDTH), lambda i, n, _: (0, clipped(n, k, blocks)))

    half = jax.ShapeDtypeStruct((8, unit, columns), BF16)
    return pl.pallas_call(
        kernel,
        out_shape=(half, half),
        grid_spec=pltpu.PrefetchScalarGridSpec(
            num_scalar_prefetch=1,
            grid=(tiles, columns // WIDTH),
            in_specs=[left_spec(k, left) for k, left in enumerate(lefts)]
            + [right_spec(k, right) for k, right in enumerate(rights)],
            out_specs=(pl.BlockSpec((per, unit, WIDTH), lambda i, n, _: (i, 0, n)),) * 2,
        ),
        compiler_params=pltpu.CompilerParams(vmem_limit_bytes=60 << 20),
        cost_estimate=HINT,
        name=name,
    )(core, *lefts, *rights)


def head_window(head):
    start = head * HEAD_DIM
    first = start // LANES * LANES
    size = LANES if start + HEAD_DIM <= first + LANES else 2 * LANES
    return first, size, start - first


def head_mask(size, offset):
    lane = lax.broadcasted_iota(jnp.int32, (1, size), 1)
    return (lane >= offset) & (lane < offset + HEAD_DIM)


def head_groups(width, slots):
    heads = [(head,) + head_window(head) for head in range(width // HEAD_DIM)]
    count = max(1, 2048 // slots)
    return [heads[i : i + count] for i in range(0, len(heads), count)]


def masked(ref, first, size, offset):
    return jnp.where(head_mask(size, offset), ref[:, first : first + size], 0)


def place(ref, start, size, offset, result):
    result = result.astype(BF16)
    if offset:
        result = jnp.where(
            head_mask(size, offset), result, ref[:, start : start + size]
        )
    ref[:, start : start + size] = result


def attend_kernel(lengths, qkv, mixed, probs_out):
    slots, width = mixed.shape
    live = lax.broadcasted_iota(jnp.int32, (1, slots), 1) < lengths[pl.program_id(0)]
    for group in head_groups(width, slots):
        scores = [
            against(
                masked(qkv, first, size, offset),
                qkv[:, width + first : width + first + size],
            )
            for _, first, size, offset in group
        ]
        scores = [jnp.where(live, s * HEAD_DIM ** (-0.5), NEG) for s in scores]
        raised = [jnp.exp(s - jnp.max(s, -1, keepdims=True)) for s in scores]
        probs = [
            (r * (1.0 / jnp.sum(r, -1, keepdims=True))).astype(BF16) for r in raised
        ]
        results = [
            simple(p, qkv[:, 2 * width + first : 2 * width + first + size])
            for p, (_, first, size, _) in zip(probs, group)
        ]
        for p, result, (head, first, size, offset) in zip(probs, results, group):
            probs_out[head * slots : (head + 1) * slots, :] = p
            place(mixed, first, size, offset, result)


def attend(qkv, lengths):
    per = lengths.shape[0]
    rows, width = qkv.shape[0], qkv.shape[1] // 3
    slots, heads = rows // per, width // HEAD_DIM
    return pl.pallas_call(
        attend_kernel,
        out_shape=(
            jax.ShapeDtypeStruct((rows, width), BF16),
            jax.ShapeDtypeStruct((rows * heads, slots), BF16),
        ),
        grid_spec=pltpu.PrefetchScalarGridSpec(
            num_scalar_prefetch=1,
            grid=(per,),
            in_specs=[pl.BlockSpec((slots, 3 * width), lambda i, _: (i, 0))],
            out_specs=(
                pl.BlockSpec((slots, width), lambda i, _: (i, 0)),
                pl.BlockSpec((heads * slots, slots), lambda i, _: (i, 0)),
            ),
        ),
        compiler_params=pltpu.CompilerParams(vmem_limit_bytes=60 << 20),
        cost_estimate=HINT,
        name="attend",
    )(lengths, qkv)


def attend_back_kernel(qkv, probs_in, grad_mixed, grad_qkv):
    slots, width = grad_mixed.shape
    scale = HEAD_DIM ** (-0.5)
    for group in head_groups(width, slots):
        grads = [masked(grad_mixed, *window) for _, *window in group]
        grad_probs = [
            against(g, qkv[:, 2 * width + first : 2 * width + first + size])
            for g, (_, first, size, _) in zip(grads, group)
        ]
        probs = [
            probs_in[head * slots : (head + 1) * slots, :] for head, _, _, _ in group
        ]
        grad_values = [across(p, g) for p, g in zip(probs, grads)]
        probs = [p.astype(F32) for p in probs]
        sums = [
            jnp.sum(g * p, -1, keepdims=True) for g, p in zip(grad_probs, probs)
        ]
        scores = [
            (p * (g - total)).astype(BF16)
            for p, g, total in zip(probs, grad_probs, sums)
        ]
        grad_queries = [
            simple(s, qkv[:, width + first : width + first + size]) * scale
            for s, (_, first, size, _) in zip(scores, group)
        ]
        grad_keys = [
            across(s, qkv[:, first : first + size]) * scale
            for s, (_, first, size, _) in zip(scores, group)
        ]
        for part, results in enumerate((grad_queries, grad_keys, grad_values)):
            for result, (_, first, size, offset) in zip(results, group):
                place(grad_qkv, part * width + first, size, offset, result)


def attend_back(qkv, probs, grad_mixed, per):
    rows, width = grad_mixed.shape
    slots, heads = rows // per, width // HEAD_DIM
    return pl.pallas_call(
        attend_back_kernel,
        out_shape=jax.ShapeDtypeStruct((rows, 3 * width), BF16),
        grid=(per,),
        in_specs=[
            pl.BlockSpec((slots, 3 * width), lambda i: (i, 0)),
            pl.BlockSpec((heads * slots, slots), lambda i: (i, 0)),
            pl.BlockSpec((slots, width), lambda i: (i, 0)),
        ],
        out_specs=pl.BlockSpec((slots, 3 * width), lambda i: (i, 0)),
        compiler_params=pltpu.CompilerParams(vmem_limit_bytes=60 << 20),
        cost_estimate=HINT,
        name="attend_back",
    )(qkv, probs, grad_mixed)


def per_device(
    latents,
    skip_store,
    lengths,
    cotangent,
    skip_weight,
    skip_bias,
    first_gain,
    first_shift,
    inward_weight,
    outward_weight,
    outward_bias,
    second_gain,
    second_shift,
    expand_weight,
    expand_bias,
    contract_weight,
    contract_bias,
):
    items, slot_dev, width = latents.shape
    ways, side = lax.axis_size("seq"), lax.axis_index("seq")
    slots = slot_dev * ways
    per = -(-items // ways)
    rows = per * slots
    fast = fast_mesh()
    chain = Chain()

    live = jnp.pad(lengths, (0, per * ways - items), constant_values=slots)
    live = pick(live, side, per)

    small = (
        skip_bias,
        first_gain,
        first_shift,
        outward_bias,
        second_gain,
        second_shift,
        expand_bias,
        contract_bias,
    )
    if fast:
        skip_piece = flip(chain.run(eighth, skip_weight), "seq")
        attention_piece = flip(
            chain.run(
                lambda a, b: jnp.concatenate([eighth(a), eighth(b)], 1),
                inward_weight,
                outward_weight,
            ),
            "seq",
        )
        vectors = gather_vectors(chain, small)
        expand_piece = flip(chain.run(eighth, expand_weight), "seq")
        skip_pieces = chain.run(lambda a: start_items(a, per), skip_store)
        latent_pieces = chain.run(lambda a: start_items(a, per), latents)
        skip_parts = (skip_weight, share(*chain.enter(skip_piece)))
        attention_other = share(*chain.enter(attention_piece))
        inward_parts = (inward_weight, attention_other)
        outward_parts = (outward_weight, attention_other)
        grad_pieces = chain.run(lambda a: split_items(a, per), cotangent)
        skip_rows = chain.run(
            lambda *a: joined_pieces(a, 2).reshape(rows, width), *skip_pieces
        )
        skip_base = chain.run(
            lambda a: dense(
                "skip_base", skip_base_body, (a,), (), ((1, 1, skip_parts),), [(width, F32)]
            )[0],
            skip_rows,
        )
        expand_parts = (expand_weight, share(*chain.enter(expand_piece)))
        contract_piece = chain.run(eighth_copy, contract_weight)
        latent_rows = chain.run(
            lambda *a: joined_pieces(a, 1).reshape(rows, width), *latent_pieces
        )
        contract_piece = flip(*chain.enter(contract_piece), "seq")
        grad_pieces = swap_pieces(chain.enter(*grad_pieces))
    else:
        skip_parts, inward_parts, outward_parts, expand_parts, contract_parts = (
            (lax.all_gather(shard, "seq", axis=0, tiled=True),)
            for shard in (
                skip_weight,
                inward_weight,
                outward_weight,
                expand_weight,
                contract_weight,
            )
        )
        skip_rows = joined_pieces(start_items(skip_store, per), 2)
        latent_rows = joined_pieces(start_items(latents, per), 1)
        grad_pieces = start_items(cotangent, per)
        vectors = gather_vectors(chain, small)
    (
        skip_offset,
        gain_first,
        shift_first,
        outward_offset,
        gain_second,
        shift_second,
        expand_offset,
        contract_offset,
    ) = vectors
    skip_matrix, inward_matrix = (2, 0, skip_parts), (3, 0, inward_parts)
    outward_matrix = (1, 3 if fast else 0, outward_parts)
    skip_rows, latent_rows = (a.reshape(rows, width) for a in (skip_rows, latent_rows))
    if not fast:
        skip_base = chain.run(
            lambda a: dense(
                "skip_base", skip_base_body, (a,), (), ((1, 1, skip_parts),), [(width, F32)]
            )[0],
            skip_rows,
        )
    one, wide = (width, BF16), (width, F32)
    hidden = (expand_offset.shape[1], BF16)

    base, first_normed, qkv_vals = chain.run(
        lambda *a: dense(
            "base_inward",
            base_inward_body,
            a,
            (skip_offset, gain_first, shift_first),
            ((1, 0, skip_parts), inward_matrix),
            [wide, one, (3 * width, BF16)],
        ),
        latent_rows,
        skip_base,
    )
    mixed_rows, probs = chain.run(lambda a: attend(a, live), qkv_vals)
    if fast:
        contract_parts = (contract_weight, share(*chain.enter(contract_piece)))
    expand_matrix, contract_matrix = (4, 0, expand_parts), (4, 0, contract_parts)
    middle, second_normed, activated, slope = chain.run(
        lambda *a: dense(
            "middle_expand",
            middle_expand_body,
            a,
            (outward_offset, gain_second, shift_second, expand_offset),
            (outward_matrix, expand_matrix),
            [wide, one, hidden, hidden],
            steps=4,
        ),
        mixed_rows,
        base,
    )
    grad_out = chain.run(
        lambda *a: joined_pieces(a, 1).reshape(rows, width), *grad_pieces
    )
    contract_sum = Reduction(chain, "contract_grad", (activated,), (grad_out,))
    grad_upper, grad_expand_off, grad_contract_off = chain.run(
        lambda *a: dense(
            "upper_back",
            upper_back_body,
            a,
            (),
            (contract_matrix,),
            [hidden],
            [hidden[0], width],
        ),
        grad_out,
        slope,
    )
    contract_sum.step()
    expand_sum = Reduction(chain, "expand_grad", (second_normed,), (grad_upper,))
    (
        grad_branch,
        grad_middle,
        grad_mixed,
        grad_gain_two,
        grad_shift_two,
        grad_outward_off,
    ) = chain.run(
        lambda *a: dense(
            "middle_back",
            functools.partial(norm_back_body, 4),
            a,
            (gain_second,),
            (expand_matrix, outward_matrix),
            [one, wide, one],
            [width] * 3,
        ),
        grad_upper,
        middle,
        grad_out,
    )
    expand_sum.step()
    contract_sum.step()
    grad_qkv = chain.run(lambda a: attend_back(qkv_vals, probs, a, per), grad_mixed)
    attention_sum = Reduction(
        chain,
        "attention_grad",
        (first_normed, mixed_rows),
        (grad_qkv, grad_branch),
        lanes=2,
    )
    contract_sum.step()
    grad_base, grad_gain_one, grad_shift_one, grad_skip_off = chain.run(
        lambda *a: dense(
            "base_back",
            functools.partial(norm_back_body, 3),
            a,
            (gain_first,),
            (inward_matrix,),
            [one],
            [width] * 3,
        ),
        grad_qkv,
        base,
        grad_middle,
    )
    expand_sum.step()
    contract_sum.step()
    attention_sum.step(1)
    attention_sum.step(0)
    skip_sum = Reduction(chain, "skip_grad", (latent_rows, skip_rows), (grad_base,))
    expand_sum.step()
    skip_sum.step()
    contract_sum.step()
    attention_sum.step(0)
    expand_sum.step()
    vector_sum = VectorReduction(
        chain,
        (
            grad_skip_off,
            grad_gain_one,
            grad_shift_one,
            grad_outward_off,
            grad_gain_two,
            grad_shift_two,
            grad_expand_off,
            grad_contract_off,
        ),
    )
    attention_sum.step(0)
    vector_sum.step()
    attention_sum.step(1)
    attention_sum.step(0)
    expand_sum.step()
    attention_sum.step(1)
    vector_sum.step()
    halves = ways == 2
    columns = [width] + ([width // 2] * 2 if halves else [width])
    grad_latents, *grad_skip = chain.run(
        lambda a: dense(
            "joined_back",
            against_body,
            (a,),
            (),
            (skip_matrix,),
            [(size, BF16) for size in columns],
        ),
        grad_base,
    )
    latent_pieces = chain.run(
        lambda a: split_parts(a.reshape(per, slots, width), 1), grad_latents
    )
    if halves:
        skip_pieces = chain.run(
            lambda a, b: (jnp.where(side == 0, a, b), jnp.where(side == 0, b, a)),
            *grad_skip,
        )
        skip_pieces = tuple(a.reshape(per, slots, width // 2) for a in skip_pieces)
    else:
        skip_pieces = split_parts(grad_skip[0].reshape(per, slots, width), 2)
    attention_sum.step(1)
    skip_sum.step()
    vector_sum.step()
    latent_pieces = swap_pieces(chain.enter(*latent_pieces))
    skip_pieces = swap_pieces(chain.enter(*skip_pieces))
    (sum_contract,) = contract_sum.finish()
    skip_sum.step()
    vector_sum.step()
    attention_sum.join()
    skip_sum.step()
    (result,) = chain.run(
        lambda *a: dense(
            "contract",
            contract_body,
            a,
            (contract_offset,),
            (contract_matrix,),
            [one],
            steps=4,
        ),
        activated,
        middle,
    )
    grad_latents = chain.run(
        lambda *a: joined_pieces(a, 0)[:items].astype(F32), *latent_pieces
    )
    skip_sum.step()
    grad_skip = chain.run(lambda *a: joined_pieces(a, 0)[:items], *skip_pieces)
    output_pieces = chain.run(
        lambda a: split_parts(a.reshape(per, slots, width), 1), result
    )
    output_pieces = swap_pieces(output_pieces)
    (sum_expand,) = expand_sum.finish()
    vector_sum.step()
    sum_inward, sum_outward = attention_sum.finish()
    (sum_skipw,) = skip_sum.finish()
    output = chain.run(lambda *a: joined_pieces(a, 0)[:items], *output_pieces)
    (
        sum_skipb,
        sum_gain1,
        sum_shift1,
        sum_outb,
        sum_gain2,
        sum_shift2,
        sum_expandb,
        sum_contractb,
    ) = vector_sum.finish()
    return (
        output,
        grad_latents,
        grad_skip,
        sum_skipw,
        sum_skipb,
        sum_gain1,
        sum_shift1,
        sum_inward,
        sum_outward,
        sum_outb,
        sum_gain2,
        sum_shift2,
        sum_expand,
        sum_expandb,
        sum_contract,
        sum_contractb,
    )


def solution(mesh):
    wide, seq = mesh.shape["wide"], mesh.shape["seq"]
    devices = mesh.devices.reshape(wide // 8, 2, 2, 2, seq)
    return jax.shard_map(
        per_device,
        mesh=Mesh(devices, WIDE + ("seq",)),
        in_specs=(
            P(WIDE, "seq", None),
            P(WIDE, None, "seq"),
            P(WIDE),
            P(WIDE, "seq", None),
            P("seq", None),
            P("seq"),
            P("seq"),
            P("seq"),
            P("seq", None),
            P("seq", None),
            P("seq"),
            P("seq"),
            P("seq"),
            P("seq", None),
            P("seq"),
            P("seq", None),
            P("seq"),
        ),
        out_specs=(
            P(WIDE, "seq", None),
            P(WIDE, "seq", None),
            P(WIDE, None, "seq"),
            P("seq", None),
            P("seq"),
            P("seq"),
            P("seq"),
            P("seq", None),
            P("seq", None),
            P("seq"),
            P("seq"),
            P("seq"),
            P("seq", None),
            P("seq"),
            P("seq", None),
            P("seq"),
        ),
        check_vma=False,
    )
```

```python
import functools

import jax
import jax.numpy as jnp
from jax import lax
from jax.experimental import pallas as pl
from jax.experimental.pallas import tpu as pltpu
from jax.sharding import Mesh
from jax.sharding import PartitionSpec as P

HEAD_DIM = 72
WIDTH = 16 * HEAD_DIM

EPS = 1e-05
NEG = -1e30
PLANE = ("z", "x", "c")
WIDE = ("w",) + PLANE
BF16 = jnp.bfloat16
F32 = jnp.float32
LANES = 128

def across(left_side, right_side):
    return lax.dot_general(
        left_side, right_side, (((0,), (0,)), ((), ())), preferred_element_type=F32
    )


def against(left_side, right_side):
    return lax.dot_general(
        left_side, right_side, (((1,), (1,)), ((), ())), preferred_element_type=F32
    )


def simple(left_side, right_side):
    return jnp.dot(left_side, right_side, preferred_element_type=F32)


def pick(array, index, size, axis=0):
    return lax.dynamic_slice_in_dim(array, index * size, size, axis)


def flip(array, axis):
    return lax.ppermute(array, axis, [(0, 1), (1, 0)])


def ordered(mine, other, index, axis=0):
    return jnp.where(
        index == 0,
        jnp.concatenate([mine, other], axis),
        jnp.concatenate([other, mine], axis),
    )


class Chain:
    def __init__(self):
        self.last = ()

    def enter(self, *values):
        values = lax.optimization_barrier(values + self.last)[: len(values)]
        return values

    def leave(self, *values):
        self.last = values[:1]
        return values if len(values) > 1 else values[0]

    def run(self, function, *values):
        out = function(*self.enter(*values))
        self.last = tuple(out)[:1] if isinstance(out, (tuple, list)) else (out,)
        return out


def fast_mesh():
    return lax.axis_size("seq") == 2 and lax.axis_size("w") == 2


def block(array, index, axis):
    return lax.dynamic_index_in_dim(array, index, axis, keepdims=False)


def eighth(shard):
    place = lax.axis_index("z") * 4 + lax.axis_index("x") * 2 + lax.axis_index("c")
    return pick(shard, place, shard.shape[0] // 8)


def share(piece):
    return lax.all_gather(piece, PLANE, axis=0, tiled=True)


class Reduction:
    def __init__(self, chain, name, lefts, rights, lanes=1):
        self.chain, self.lanes = chain, lanes
        self.cuts = [right.shape[1] for right in rights]
        if fast_mesh():
            core = lax.axis_index("c").reshape(1)
            count = len(lefts)
            sent, keep = chain.run(
                lambda *a: core_gradients(name, core, a[:count], a[count:]),
                *lefts,
                *rights,
            )
            self.parts = [(keep, flip(sent, "c"))] * lanes
            self.names = [["seq", "x", "z", "w"] for _ in range(lanes)]
        else:
            axis = int(len(rights) > 1)
            pairs = zip(lefts, rights) if axis else ((a, rights[0]) for a in lefts)
            grad = jnp.concatenate([across(*p).astype(BF16) for p in pairs], axis)
            part = lax.psum_scatter(grad, "seq", scatter_dimension=0, tiled=True)
            self.total, self.names = lax.psum(part, WIDE), None

    def step(self, lane=0):
        if self.names is None:
            return
        if not self.names[lane]:
            self.join()
            return
        name, parts = self.names[lane].pop(0), self.parts[lane]
        if name == "w":
            sent = self.chain.run(
                lambda *a: add(*(part.reshape(part.shape[1:]) for part in a)), *parts
            )
            self.parts[lane] = (sent, flip(sent, name))
        else:
            outer = 2 if name == "x" else 1
            lanes = self.lanes if name == "seq" else 1
            sent, keep = self.chain.run(
                functools.partial(fold, name, outer, lane if lanes > 1 else 0, lanes),
                *parts,
            )
            self.parts[lane] = (keep, flip(sent, name))

    def join(self):
        if self.names is None:
            return
        assert not any(self.names)
        parts = [part for pair in self.parts for part in pair]
        self.total = share(self.chain.run(add, *parts))

    def finish(self):
        return self.chain.run(functools.partial(widen, self.cuts), self.total)


def gather_vectors(chain, vectors):
    joined = chain.run(lambda *a: jnp.concatenate(a), *vectors)
    mine = joined.reshape(1, -1)
    if fast_mesh():
        everything = ordered(mine, flip(mine, "seq"), lax.axis_index("seq"))
    else:
        everything = lax.all_gather(mine, "seq", axis=0, tiled=True)
    out, start = [], 0
    for vector in vectors:
        size = vector.shape[0]
        out.append(everything[:, start : start + size].reshape(1, -1).astype(F32))
        start += size
    return out


class VectorReduction:
    def __init__(self, chain, vectors):
        self.chain, self.sizes = chain, [vector.shape[1] for vector in vectors]
        self.total = chain.run(lambda *a: jnp.concatenate(a, 1), *vectors)
        self.names = ["c", "x", "z", "w", "seq"]
        if fast_mesh():
            self.got = flip(self.total, self.names.pop(0))
        else:
            self.total, self.names = lax.psum(self.total, WIDE + ("seq",)), []

    def step(self):
        if fast_mesh():
            self.total = self.chain.run(add, self.total, self.got)
            if self.names:
                self.got = flip(self.total, self.names.pop(0))

    def finish(self):
        assert not self.names
        ways, side = lax.axis_size("seq"), lax.axis_index("seq")
        out, start = [], 0
        for whole in self.sizes:
            size = whole // ways
            shards = self.total[:, start : start + whole].reshape(ways, size)
            out.append(block(shards, side, 0))
            start += whole
        return out


def split_items(array, per):
    ways, side = lax.axis_size("seq"), lax.axis_index("seq")
    padding = [(0, per * ways - array.shape[0])] + [(0, 0)] * (array.ndim - 1)
    array = jnp.pad(array, padding)
    return tuple(pick(array, (side + hop) % ways, per) for hop in range(ways))


def split_parts(whole, axis):
    ways, side = lax.axis_size("seq"), lax.axis_index("seq")
    size = whole.shape[axis] // ways
    return tuple(pick(whole, (side + hop) % ways, size, axis) for hop in range(ways))


def swap_pieces(pieces):
    ways = lax.axis_size("seq")
    return pieces[:1] + tuple(
        lax.ppermute(piece, "seq", [(i, (i + hop) % ways) for i in range(ways)])
        for hop, piece in enumerate(pieces)
        if hop
    )


def start_items(array, per):
    return swap_pieces(split_items(array, per))


def joined_pieces(pieces, axis):
    ways, side = lax.axis_size("seq"), lax.axis_index("seq")
    if ways == 2:
        return ordered(pieces[0], pieces[1], side, axis)
    size = pieces[0].shape[axis]
    shape = list(pieces[0].shape)
    shape[axis] = size * ways
    whole = jnp.zeros(shape, pieces[0].dtype)
    for hop, piece in enumerate(pieces):
        source = (side - hop) % ways
        whole = lax.dynamic_update_slice_in_dim(whole, piece, source * size, axis)
    return whole


HINT = pl.CostEstimate(flops=10**13, transcendentals=0, bytes_accessed=10**9)


def block_loader(parts, offset, blocks, base, count, side, sems):
    size = blocks.shape[1]
    rows, columns = parts[0].shape
    first = pl.program_id(0) == 0
    copies = []
    for b in range(count):
        copies.append([])
        target = base + b
        if len(parts) == 1:
            row, column = divmod(b + offset, columns // size)
            source = parts[0].at[pl.ds(row * size, size), pl.ds(column * size, size)]
            copy = pltpu.make_async_copy(source, blocks.at[target], sems.at[0, target])
            copies[b].append((first, copy))
        elif rows >= size:
            half, place = divmod(b + offset, rows // size)
            for p, part in enumerate(parts):
                mine = side == half if p == 0 else side != half
                source = part.at[pl.ds(place * size, size), :]
                copy = pltpu.make_async_copy(
                    source, blocks.at[target], sems.at[0, target]
                )
                copies[b].append((jnp.logical_and(first, mine), copy))
        else:
            for p, part in enumerate(parts):
                start = pl.multiple_of((side if p == 0 else 1 - side) * rows, 16)
                column = (b + (offset if p else 0)) * size
                copy = pltpu.make_async_copy(
                    part.at[:, pl.ds(column, size)],
                    blocks.at[target, pl.ds(start, rows), :],
                    sems.at[p, target],
                )
                copies[b].append((first, copy))
    for pair in copies:
        for when, copy in pair:
            pl.when(when)(copy.start)
    return copies


def dense(name, body, rows_in, vectors, weights, outs, sums=(), steps=2):
    rows = rows_in[0].shape[0]
    tile = rows // steps
    total = sum(count for count, _, _ in weights)
    arrays = [part for _, _, parts in weights for part in parts]
    cuts = [len(rows_in), len(vectors), len(arrays), len(outs), len(sums)]

    def kernel(side, *refs):
        groups = []
        for size in cuts:
            groups.append(refs[:size])
            refs = refs[size:]
        blocks, sems = refs
        copies, parts = [], groups[2]
        for count, offset, used in weights:
            copies += block_loader(
                parts[: len(used)], offset, blocks, len(copies), count, side[0], sems
            )
            parts = parts[len(used) :]

        def wait(b):
            for when, copy in copies[b]:
                pl.when(when)(copy.wait)

        if sums:

            @pl.when(pl.program_id(0) == 0)
            def _():
                for ref in groups[4]:
                    ref[...] = jnp.zeros_like(ref)

        body(wait, blocks, groups[0], groups[1], groups[3], groups[4])

    return pl.pallas_call(
        kernel,
        out_shape=tuple(jax.ShapeDtypeStruct((rows, c), d) for c, d in outs)
        + tuple(jax.ShapeDtypeStruct((1, c), F32) for c in sums),
        grid_spec=pltpu.PrefetchScalarGridSpec(
            num_scalar_prefetch=1,
            grid=(steps,),
            in_specs=[
                pl.BlockSpec((tile, a.shape[1]), lambda i, _: (i, 0)) for a in rows_in
            ]
            + [pl.BlockSpec(a.shape, lambda i, _: (0, 0)) for a in vectors]
            + [pl.BlockSpec(memory_space=pl.ANY) for _ in arrays],
            out_specs=tuple(pl.BlockSpec((tile, c), lambda i, _: (i, 0)) for c, _ in outs)
            + tuple(pl.BlockSpec((1, c), lambda i, _: (0, 0)) for c in sums),
            scratch_shapes=[
                pltpu.VMEM((total, WIDTH, WIDTH), BF16),
                pltpu.SemaphoreType.DMA((2, total)),
            ],
        ),
        compiler_params=pltpu.CompilerParams(vmem_limit_bytes=60 << 20),
        cost_estimate=HINT,
        name=name,
    )(lax.axis_index("seq").reshape(1), *rows_in, *vectors, *arrays)


def fold_kernel(index_ref, *refs):
    (*parts, sent, keep) = refs
    index = index_ref[0]

    def total(place):
        values = [part[0, place].astype(F32) for part in parts]
        return sum(values[1:], values[0]).astype(BF16)

    sent[0] = total(1 - index)
    keep[0] = total(index)


def fold(name, outer, lane, lanes, *parts):
    index = lax.axis_index(name).reshape(1)
    count, unit, columns = parts[0].shape
    inner = count // (2 * outer)
    size, together = columns // lanes, min(inner, 2)
    half = jax.ShapeDtypeStruct((outer, inner, unit, size), BF16)
    out = pl.pallas_call(
        fold_kernel,
        out_shape=(half, half),
        grid_spec=pltpu.PrefetchScalarGridSpec(
            num_scalar_prefetch=1,
            grid=(outer, inner // together),
            in_specs=[
                pl.BlockSpec(
                    (1, 2, together, unit, size), lambda i, j, _: (i, 0, j, 0, lane)
                )
                for _ in parts
            ],
            out_specs=(
                pl.BlockSpec((1, together, unit, size), lambda i, j, _: (i, j, 0, 0)),
            )
            * 2,
        ),
        compiler_params=pltpu.CompilerParams(vmem_limit_bytes=60 << 20),
        cost_estimate=HINT,
        name="fold_" + name,
    )(index, *(part.reshape(outer, 2, inner, unit, columns) for part in parts))
    return tuple(part.reshape(count // 2, unit, size) for part in out)


def add_kernel(*refs):
    (*parts, out) = refs
    size = parts[0].shape[1]
    for k in range(len(parts) // 2):
        total = parts[2 * k][...].astype(F32) + parts[2 * k + 1][...].astype(F32)
        out[:, k * size : (k + 1) * size] = total.astype(out.dtype)


def add(*parts):
    rows, columns = parts[0].shape
    return pl.pallas_call(
        add_kernel,
        out_shape=jax.ShapeDtypeStruct((rows, columns * len(parts) // 2), parts[0].dtype),
        compiler_params=pltpu.CompilerParams(vmem_limit_bytes=60 << 20),
        cost_estimate=HINT,
        name="add",
    )(*parts)


def widen_kernel(value, *outs):
    start = 0
    for out in outs:
        out[...] = value[:, start : start + out.shape[1]].astype(F32)
        start += out.shape[1]


def widen(cuts, value):
    rows, columns = value.shape
    steps = 2
    return pl.pallas_call(
        widen_kernel,
        out_shape=tuple(jax.ShapeDtypeStruct((rows, size), F32) for size in cuts),
        grid=(steps,),
        in_specs=[pl.BlockSpec((rows // steps, columns), lambda i: (i, 0))],
        out_specs=tuple(
            pl.BlockSpec((rows // steps, size), lambda i: (i, 0)) for size in cuts
        ),
        compiler_params=pltpu.CompilerParams(vmem_limit_bytes=60 << 20),
        cost_estimate=HINT,
        name="widen",
    )(value)


def eighth_copy_kernel(place, shard, out):
    out[...] = shard[...]


def eighth_copy(shard):
    rows, columns = shard.shape[0] // 8, shard.shape[1]
    place = lax.axis_index("z") * 4 + lax.axis_index("x") * 2 + lax.axis_index("c")
    return pl.pallas_call(
        eighth_copy_kernel,
        out_shape=jax.ShapeDtypeStruct((rows, columns), BF16),
        grid_spec=pltpu.PrefetchScalarGridSpec(
            num_scalar_prefetch=1,
            grid=(1,),
            in_specs=[pl.BlockSpec((rows, columns), lambda i, place: (place[0], 0))],
            out_specs=pl.BlockSpec((rows, columns), lambda i, place: (0, 0)),
        ),
        compiler_params=pltpu.CompilerParams(vmem_limit_bytes=60 << 20),
        cost_estimate=HINT,
        name="eighth",
    )(place.reshape(1), shard)


def normalize(hidden):
    mean_val = jnp.mean(hidden, -1, keepdims=True)
    centred = hidden - mean_val
    scale = lax.rsqrt(jnp.mean(centred * centred, -1, keepdims=True) + EPS)
    return centred * scale, scale


def add_sum(ref, values):
    ref[...] += jnp.sum(values, 0, keepdims=True)


def columns_of(b):
    return slice(b * WIDTH, (b + 1) * WIDTH)


def skip_base_body(wait, blocks, rows, vectors, outs, sums):
    wait(0)
    outs[0][...] = simple(rows[0][...], blocks[0])


def base_inward_body(wait, blocks, rows, vectors, outs, sums):
    wait(0)
    total = simple(rows[0][...], blocks[0]) + rows[1][...] + vectors[0][...]
    outs[0][...] = total
    normed = (normalize(total)[0] * vectors[1][...] + vectors[2][...]).astype(BF16)
    outs[1][...] = normed
    for b in range(3):
        wait(1 + b)
        outs[2][:, columns_of(b)] = simple(outs[1][...], blocks[1 + b]).astype(BF16)


def middle_expand_body(wait, blocks, rows, vectors, outs, sums):
    wait(0)
    total = simple(rows[0][...], blocks[0]) + rows[1][...] + vectors[0][...]
    outs[0][...] = total
    normed = (normalize(total)[0] * vectors[1][...] + vectors[2][...]).astype(BF16)
    outs[1][...] = normed
    for b in range(4):
        wait(1 + b)
        upper = simple(outs[1][...], blocks[1 + b]) + vectors[3][:, columns_of(b)]
        below = 0.5 * (1.0 + lax.erf(upper * 0.7071067811865476))
        bell = jnp.exp(-0.5 * upper * upper) * 0.3989422804014327
        outs[2][:, columns_of(b)] = (upper * below).astype(BF16)
        outs[3][:, columns_of(b)] = (below + upper * bell).astype(BF16)


def contract_body(wait, blocks, rows, vectors, outs, sums):
    total = rows[1][...] + vectors[0][...]
    for b in range(blocks.shape[0]):
        wait(b)
        total = total + simple(rows[0][:, columns_of(b)], blocks[b])
    outs[0][...] = total.astype(BF16)


def upper_back_body(wait, blocks, rows, vectors, outs, sums):
    grad = rows[0][...]
    add_sum(sums[1], grad.astype(F32))
    for b in range(blocks.shape[0]):
        wait(b)
        upper = against(grad, blocks[b]) * rows[1][:, columns_of(b)].astype(F32)
        upper = upper.astype(BF16)
        outs[0][:, columns_of(b)] = upper
        add_sum(sums[0].at[:, columns_of(b)], upper.astype(F32))


def norm_back_body(count, wait, blocks, rows, vectors, outs, sums):
    grad = None
    for b in range(count):
        wait(b)
        part = against(rows[0][:, columns_of(b)], blocks[b])
        grad = part if grad is None else grad + part
    xhat, scale = normalize(rows[1][...])
    inner = grad * vectors[0][...]
    back = scale * (
        inner
        - jnp.mean(inner, -1, keepdims=True)
        - xhat * jnp.mean(inner * xhat, -1, keepdims=True)
    )
    total = rows[2][...].astype(F32) + back
    rounded = total.astype(BF16)
    outs[0][...] = rounded
    add_sum(sums[0], grad * xhat)
    add_sum(sums[1], grad)
    add_sum(sums[2], rounded.astype(F32))
    if len(outs) > 1:
        outs[1][...] = total
        wait(count)
        outs[2][...] = against(outs[0][...], blocks[count]).astype(BF16)


def against_body(wait, blocks, rows, vectors, outs, sums):
    for b in range(blocks.shape[0]):
        wait(b)
        result = against(rows[0][...], blocks[b]).astype(BF16)
        size = outs[b].shape[1]
        outs[b][...] = result[:, :size]
        if size < WIDTH:
            outs[b + 1][...] = result[:, size:]


def core_gradients(name, core, lefts, rights):
    rows = rights[0].shape[0]
    columns = sum(right.shape[1] for right in rights)
    stacked = len(rights) == 1
    depth = sum(left.shape[1] for left in lefts) if stacked else WIDTH
    tiles, unit = depth // WIDTH, depth // 16
    per = WIDTH // unit // 2
    count = len(lefts)
    ends = [0]
    for array in lefts if stacked else rights:
        ends.append(ends[-1] + array.shape[1] // WIDTH)

    def kernel(core_ref, *refs):
        left, right = refs[:count], refs[count : count + len(rights)]
        sent, keep = refs[count + len(rights) :]

        def run(left_ref, right_ref):
            grad = across(left_ref[...], right_ref[...])
            second = core_ref[0] == 1
            for j in range(0, 2 * per, 2):
                even = grad[j * unit : (j + 1) * unit].astype(BF16)
                odd = grad[(j + 1) * unit : (j + 2) * unit].astype(BF16)
                keep[j // 2] = jnp.where(second, odd, even)
                sent[j // 2] = jnp.where(second, even, odd)

        if count == 1:
            run(left[0], right[0])
        else:
            place = pl.program_id(0 if stacked else 1)
            for k in range(count):
                here = jnp.logical_and(place >= ends[k], place < ends[k + 1])
                pl.when(here)(
                    functools.partial(run, left[k], right[0 if stacked else k])
                )

    def clipped(index, k, blocks):
        return jnp.clip(index - ends[k], 0, blocks - 1)

    def left_spec(k, left):
        blocks = left.shape[1] // WIDTH
        if stacked:
            return pl.BlockSpec(
                (rows, WIDTH), lambda i, n, _: (0, clipped(i, k, blocks))
            )
        return pl.BlockSpec((rows, WIDTH), lambda i, n, _: (0, 0))

    def right_spec(k, right):
        blocks = right.shape[1] // WIDTH
        if stacked:
            return pl.BlockSpec((rows, WIDTH), lambda i, n, _: (0, n))
        return pl.BlockSpec((rows, WIDTH), lambda i, n, _: (0, clipped(n, k, blocks)))

    half = jax.ShapeDtypeStruct((8, unit, columns), BF16)
    return pl.pallas_call(
        kernel,
        out_shape=(half, half),
        grid_spec=pltpu.PrefetchScalarGridSpec(
            num_scalar_prefetch=1,
            grid=(tiles, columns // WIDTH),
            in_specs=[left_spec(k, left) for k, left in enumerate(lefts)]
            + [right_spec(k, right) for k, right in enumerate(rights)],
            out_specs=(pl.BlockSpec((per, unit, WIDTH), lambda i, n, _: (i, 0, n)),) * 2,
        ),
        compiler_params=pltpu.CompilerParams(vmem_limit_bytes=60 << 20),
        cost_estimate=HINT,
        name=name,
    )(core, *lefts, *rights)


def head_window(head):
    start = head * HEAD_DIM
    first = start // LANES * LANES
    size = LANES if start + HEAD_DIM <= first + LANES else 2 * LANES
    return first, size, start - first


def head_mask(size, offset):
    lane = lax.broadcasted_iota(jnp.int32, (1, size), 1)
    return (lane >= offset) & (lane < offset + HEAD_DIM)


def head_groups(width, slots):
    heads = [(head,) + head_window(head) for head in range(width // HEAD_DIM)]
    count = max(1, 2048 // slots)
    return [heads[i : i + count] for i in range(0, len(heads), count)]


def masked(ref, first, size, offset):
    return jnp.where(head_mask(size, offset), ref[:, first : first + size], 0)


def place(ref, start, size, offset, result):
    result = result.astype(BF16)
    if offset:
        result = jnp.where(
            head_mask(size, offset), result, ref[:, start : start + size]
        )
    ref[:, start : start + size] = result


def attend_kernel(lengths, qkv, mixed, probs_out):
    slots, width = mixed.shape
    live = lax.broadcasted_iota(jnp.int32, (1, slots), 1) < lengths[pl.program_id(0)]
    for group in head_groups(width, slots):
        scores = [
            against(
                masked(qkv, first, size, offset),
                qkv[:, width + first : width + first + size],
            )
            for _, first, size, offset in group
        ]
        scores = [jnp.where(live, s * HEAD_DIM ** (-0.5), NEG) for s in scores]
        raised = [jnp.exp(s - jnp.max(s, -1, keepdims=True)) for s in scores]
        probs = [
            (r * (1.0 / jnp.sum(r, -1, keepdims=True))).astype(BF16) for r in raised
        ]
        results = [
            simple(p, qkv[:, 2 * width + first : 2 * width + first + size])
            for p, (_, first, size, _) in zip(probs, group)
        ]
        for p, result, (head, first, size, offset) in zip(probs, results, group):
            probs_out[head * slots : (head + 1) * slots, :] = p
            place(mixed, first, size, offset, result)


def attend(qkv, lengths):
    per = lengths.shape[0]
    rows, width = qkv.shape[0], qkv.shape[1] // 3
    slots, heads = rows // per, width // HEAD_DIM
    return pl.pallas_call(
        attend_kernel,
        out_shape=(
            jax.ShapeDtypeStruct((rows, width), BF16),
            jax.ShapeDtypeStruct((rows * heads, slots), BF16),
        ),
        grid_spec=pltpu.PrefetchScalarGridSpec(
            num_scalar_prefetch=1,
            grid=(per,),
            in_specs=[pl.BlockSpec((slots, 3 * width), lambda i, _: (i, 0))],
            out_specs=(
                pl.BlockSpec((slots, width), lambda i, _: (i, 0)),
                pl.BlockSpec((heads * slots, slots), lambda i, _: (i, 0)),
            ),
        ),
        compiler_params=pltpu.CompilerParams(vmem_limit_bytes=60 << 20),
        cost_estimate=HINT,
        name="attend",
    )(lengths, qkv)


def attend_back_kernel(qkv, probs_in, grad_mixed, grad_qkv):
    slots, width = grad_mixed.shape
    scale = HEAD_DIM ** (-0.5)
    for group in head_groups(width, slots):
        grads = [masked(grad_mixed, *window) for _, *window in group]
        grad_probs = [
            against(g, qkv[:, 2 * width + first : 2 * width + first + size])
            for g, (_, first, size, _) in zip(grads, group)
        ]
        probs = [
            probs_in[head * slots : (head + 1) * slots, :] for head, _, _, _ in group
        ]
        grad_values = [across(p, g) for p, g in zip(probs, grads)]
        probs = [p.astype(F32) for p in probs]
        sums = [
            jnp.sum(g * p, -1, keepdims=True) for g, p in zip(grad_probs, probs)
        ]
        scores = [
            (p * (g - total)).astype(BF16)
            for p, g, total in zip(probs, grad_probs, sums)
        ]
        grad_queries = [
            simple(s, qkv[:, width + first : width + first + size]) * scale
            for s, (_, first, size, _) in zip(scores, group)
        ]
        grad_keys = [
            across(s, qkv[:, first : first + size]) * scale
            for s, (_, first, size, _) in zip(scores, group)
        ]
        for part, results in enumerate((grad_queries, grad_keys, grad_values)):
            for result, (_, first, size, offset) in zip(results, group):
                place(grad_qkv, part * width + first, size, offset, result)


def attend_back(qkv, probs, grad_mixed, per):
    rows, width = grad_mixed.shape
    slots, heads = rows // per, width // HEAD_DIM
    return pl.pallas_call(
        attend_back_kernel,
        out_shape=jax.ShapeDtypeStruct((rows, 3 * width), BF16),
        grid=(per,),
        in_specs=[
            pl.BlockSpec((slots, 3 * width), lambda i: (i, 0)),
            pl.BlockSpec((heads * slots, slots), lambda i: (i, 0)),
            pl.BlockSpec((slots, width), lambda i: (i, 0)),
        ],
        out_specs=pl.BlockSpec((slots, 3 * width), lambda i: (i, 0)),
        compiler_params=pltpu.CompilerParams(vmem_limit_bytes=60 << 20),
        cost_estimate=HINT,
        name="attend_back",
    )(qkv, probs, grad_mixed)


def per_device(
    latents,
    skip_store,
    lengths,
    cotangent,
    skip_weight,
    skip_bias,
    first_gain,
    first_shift,
    inward_weight,
    outward_weight,
    outward_bias,
    second_gain,
    second_shift,
    expand_weight,
    expand_bias,
    contract_weight,
    contract_bias,
):
    items, slot_dev, width = latents.shape
    ways, side = lax.axis_size("seq"), lax.axis_index("seq")
    slots = slot_dev * ways
    per = -(-items // ways)
    rows = per * slots
    fast = fast_mesh()
    chain = Chain()

    live = jnp.pad(lengths, (0, per * ways - items), constant_values=slots)
    live = pick(live, side, per)

    small = (
        skip_bias,
        first_gain,
        first_shift,
        outward_bias,
        second_gain,
        second_shift,
        expand_bias,
        contract_bias,
    )
    if fast:
        skip_piece = flip(chain.run(eighth, skip_weight), "seq")
        attention_piece = flip(
            chain.run(
                lambda a, b: jnp.concatenate([eighth(a), eighth(b)], 1),
                inward_weight,
                outward_weight,
            ),
            "seq",
        )
        vectors = gather_vectors(chain, small)
        expand_piece = flip(chain.run(eighth, expand_weight), "seq")
        skip_pieces = chain.run(lambda a: start_items(a, per), skip_store)
        latent_pieces = chain.run(lambda a: start_items(a, per), latents)
        skip_parts = (skip_weight, share(*chain.enter(skip_piece)))
        attention_other = share(*chain.enter(attention_piece))
        inward_parts = (inward_weight, attention_other)
        outward_parts = (outward_weight, attention_other)
        grad_pieces = chain.run(lambda a: split_items(a, per), cotangent)
        skip_rows = chain.run(
            lambda *a: joined_pieces(a, 2).reshape(rows, width), *skip_pieces
        )
        skip_base = chain.run(
            lambda a: dense(
                "skip_base", skip_base_body, (a,), (), ((1, 1, skip_parts),), [(width, F32)]
            )[0],
            skip_rows,
        )
        expand_parts = (expand_weight, share(*chain.enter(expand_piece)))
        contract_piece = chain.run(eighth_copy, contract_weight)
        latent_rows = chain.run(
            lambda *a: joined_pieces(a, 1).reshape(rows, width), *latent_pieces
        )
        contract_piece = flip(*chain.enter(contract_piece), "seq")
        grad_pieces = swap_pieces(chain.enter(*grad_pieces))
    else:
        skip_parts, inward_parts, outward_parts, expand_parts, contract_parts = (
            (lax.all_gather(shard, "seq", axis=0, tiled=True),)
            for shard in (
                skip_weight,
                inward_weight,
                outward_weight,
                expand_weight,
                contract_weight,
            )
        )
        skip_rows = joined_pieces(start_items(skip_store, per), 2)
        latent_rows = joined_pieces(start_items(latents, per), 1)
        grad_pieces = start_items(cotangent, per)
        vectors = gather_vectors(chain, small)
    (
        skip_offset,
        gain_first,
        shift_first,
        outward_offset,
        gain_second,
        shift_second,
        expand_offset,
        contract_offset,
    ) = vectors
    skip_matrix, inward_matrix = (2, 0, skip_parts), (3, 0, inward_parts)
    outward_matrix = (1, 3 if fast else 0, outward_parts)
    skip_rows, latent_rows = (a.reshape(rows, width) for a in (skip_rows, latent_rows))
    if not fast:
        skip_base = chain.run(
            lambda a: dense(
                "skip_base", skip_base_body, (a,), (), ((1, 1, skip_parts),), [(width, F32)]
            )[0],
            skip_rows,
        )
    one, wide = (width, BF16), (width, F32)
    hidden = (expand_offset.shape[1], BF16)

    base, first_normed, qkv_vals = chain.run(
        lambda *a: dense(
            "base_inward",
            base_inward_body,
            a,
            (skip_offset, gain_first, shift_first),
            ((1, 0, skip_parts), inward_matrix),
            [wide, one, (3 * width, BF16)],
        ),
        latent_rows,
        skip_base,
    )
    mixed_rows, probs = chain.run(lambda a: attend(a, live), qkv_vals)
    if fast:
        contract_parts = (contract_weight, share(*chain.enter(contract_piece)))
    expand_matrix, contract_matrix = (4, 0, expand_parts), (4, 0, contract_parts)
    middle, second_normed, activated, slope = chain.run(
        lambda *a: dense(
            "middle_expand",
            middle_expand_body,
            a,
            (outward_offset, gain_second, shift_second, expand_offset),
            (outward_matrix, expand_matrix),
            [wide, one, hidden, hidden],
            steps=4,
        ),
        mixed_rows,
        base,
    )
    grad_out = chain.run(
        lambda *a: joined_pieces(a, 1).reshape(rows, width), *grad_pieces
    )
    contract_sum = Reduction(chain, "contract_grad", (activated,), (grad_out,))
    grad_upper, grad_expand_off, grad_contract_off = chain.run(
        lambda *a: dense(
            "upper_back",
            upper_back_body,
            a,
            (),
            (contract_matrix,),
            [hidden],
            [hidden[0], width],
        ),
        grad_out,
        slope,
    )
    contract_sum.step()
    expand_sum = Reduction(chain, "expand_grad", (second_normed,), (grad_upper,))
    (
        grad_branch,
        grad_middle,
        grad_mixed,
        grad_gain_two,
        grad_shift_two,
        grad_outward_off,
    ) = chain.run(
        lambda *a: dense(
            "middle_back",
            functools.partial(norm_back_body, 4),
            a,
            (gain_second,),
            (expand_matrix, outward_matrix),
            [one, wide, one],
            [width] * 3,
        ),
        grad_upper,
        middle,
        grad_out,
    )
    expand_sum.step()
    contract_sum.step()
    grad_qkv = chain.run(lambda a: attend_back(qkv_vals, probs, a, per), grad_mixed)
    attention_sum = Reduction(
        chain,
        "attention_grad",
        (first_normed, mixed_rows),
        (grad_qkv, grad_branch),
        lanes=2,
    )
    contract_sum.step()
    grad_base, grad_gain_one, grad_shift_one, grad_skip_off = chain.run(
        lambda *a: dense(
            "base_back",
            functools.partial(norm_back_body, 3),
            a,
            (gain_first,),
            (inward_matrix,),
            [one],
            [width] * 3,
        ),
        grad_qkv,
        base,
        grad_middle,
    )
    expand_sum.step()
    contract_sum.step()
    attention_sum.step(1)
    attention_sum.step(0)
    skip_sum = Reduction(chain, "skip_grad", (latent_rows, skip_rows), (grad_base,))
    expand_sum.step()
    skip_sum.step()
    contract_sum.step()
    attention_sum.step(0)
    expand_sum.step()
    vector_sum = VectorReduction(
        chain,
        (
            grad_skip_off,
            grad_gain_one,
            grad_shift_one,
            grad_outward_off,
            grad_gain_two,
            grad_shift_two,
            grad_expand_off,
            grad_contract_off,
        ),
    )
    attention_sum.step(0)
    vector_sum.step()
    attention_sum.step(1)
    attention_sum.step(0)
    expand_sum.step()
    attention_sum.step(1)
    vector_sum.step()
    halves = ways == 2
    columns = [width] + ([width // 2] * 2 if halves else [width])
    grad_latents, *grad_skip = chain.run(
        lambda a: dense(
            "joined_back",
            against_body,
            (a,),
            (),
            (skip_matrix,),
            [(size, BF16) for size in columns],
        ),
        grad_base,
    )
    latent_pieces = chain.run(
        lambda a: split_parts(a.reshape(per, slots, width), 1), grad_latents
    )
    if halves:
        skip_pieces = chain.run(
            lambda a, b: (jnp.where(side == 0, a, b), jnp.where(side == 0, b, a)),
            *grad_skip,
        )
        skip_pieces = tuple(a.reshape(per, slots, width // 2) for a in skip_pieces)
    else:
        skip_pieces = split_parts(grad_skip[0].reshape(per, slots, width), 2)
    attention_sum.step(1)
    skip_sum.step()
    vector_sum.step()
    latent_pieces = swap_pieces(chain.enter(*latent_pieces))
    skip_pieces = swap_pieces(chain.enter(*skip_pieces))
    (sum_contract,) = contract_sum.finish()
    skip_sum.step()
    vector_sum.step()
    attention_sum.join()
    skip_sum.step()
    (result,) = chain.run(
        lambda *a: dense(
            "contract",
            contract_body,
            a,
            (contract_offset,),
            (contract_matrix,),
            [one],
            steps=4,
        ),
        activated,
        middle,
    )
    output_pieces = chain.run(
        lambda a: split_parts(a.reshape(per, slots, width), 1), result
    )
    output_pieces = swap_pieces(output_pieces)
    grad_latents = chain.run(
        lambda *a: joined_pieces(a, 0)[:items].astype(F32), *latent_pieces
    )
    skip_sum.step()
    grad_skip = chain.run(lambda *a: joined_pieces(a, 0)[:items], *skip_pieces)
    (sum_expand,) = expand_sum.finish()
    vector_sum.step()
    sum_inward, sum_outward = attention_sum.finish()
    output = chain.run(lambda *a: joined_pieces(a, 0)[:items], *output_pieces)
    (sum_skipw,) = skip_sum.finish()
    (
        sum_skipb,
        sum_gain1,
        sum_shift1,
        sum_outb,
        sum_gain2,
        sum_shift2,
        sum_expandb,
        sum_contractb,
    ) = vector_sum.finish()
    return (
        output,
        grad_latents,
        grad_skip,
        sum_skipw,
        sum_skipb,
        sum_gain1,
        sum_shift1,
        sum_inward,
        sum_outward,
        sum_outb,
        sum_gain2,
        sum_shift2,
        sum_expand,
        sum_expandb,
        sum_contract,
        sum_contractb,
    )


def solution(mesh):
    wide, seq = mesh.shape["wide"], mesh.shape["seq"]
    devices = mesh.devices.reshape(wide // 8, 2, 2, 2, seq)
    return jax.shard_map(
        per_device,
        mesh=Mesh(devices, WIDE + ("seq",)),
        in_specs=(
            P(WIDE, "seq", None),
            P(WIDE, None, "seq"),
            P(WIDE),
            P(WIDE, "seq", None),
            P("seq", None),
            P("seq"),
            P("seq"),
            P("seq"),
            P("seq", None),
            P("seq", None),
            P("seq"),
            P("seq"),
            P("seq"),
            P("seq", None),
            P("seq"),
            P("seq", None),
            P("seq"),
        ),
        out_specs=(
            P(WIDE, "seq", None),
            P(WIDE, "seq", None),
            P(WIDE, None, "seq"),
            P("seq", None),
            P("seq"),
            P("seq"),
            P("seq"),
            P("seq", None),
            P("seq", None),
            P("seq"),
            P("seq"),
            P("seq"),
            P("seq", None),
            P("seq"),
            P("seq", None),
            P("seq"),
        ),
        check_vma=False,
    )
```
